32 devices in a mesh: blk: 16 (over z, y, core), grp: 2 (over x).
Axes of the slice: x: 2, y: 2, z: 4, core: 2. Of those that a mesh axis runs over, the one named last changes fastest.
Arguments:
- tracers: float32 [2, 16, 128, 256], P(None, None, 'blk', 'grp'), may hold values from -6 to 6
- velocity: float32 [2, 16, 128, 256], P(None, None, 'blk', 'grp'), may hold values from -3 to 3
- depth_levels: int32 [128, 256], P('blk', 'grp'), may hold values from 0 to 16, as said below
- vdiff: float32 [15], replicated, may hold values from 0.05 to 0.45
Outputs:
- new_tracers: float32 [2, 16, 128, 256], P(None, None, 'blk', 'grp')
- surface: float32 [128, 256], P('blk', 'grp')
- residual: float32 [128, 256], P('blk', 'grp')
The draws below stay inside these ranges and needn't reach their ends.
Inputs may be any that keep to these rules, and one draw needn't show every extreme that they name: `depth_levels`: 16 and 0 are both reached in every draw.
All inputs are finite; a program needn't handle non-finite values.
Results may differ from the reference program's by a relative error of at most 0.0003.
Values sent between devices are 32-bit elements; how exact they have to be, the bound alone decides.
No kernel may reach another device: no remote copies, remote signals or barrier semaphores. Data moves between devices by JAX's collectives and lax.ppermute only.
A program may use at most 64 MiB of HBM per device.

```python
import math
import jax
import jax.numpy as jnp

LEV = 16
ITERS = 3
NX = 256
NY = 128


def draw_depth_levels(key, part):
    key_land = jax.random.fold_in(key, 11)
    key_deep = jax.random.fold_in(key, 23)
    land_roll = jax.random.randint(key_land, (NY, NX), 0, 10)
    deep_roll = jax.random.randint(key_deep, (NY, NX), 1, LEV + 1)
    levels_out = jnp.where(land_roll < 3, 0, deep_roll).astype(jnp.int32)
    return levels_out.at[0, 0].set(LEV).at[0, 1].set(0)


def level_of(key, extent, split, low, high):
    def one(dim, shards_of):
        heights = jax.random.uniform(jax.random.fold_in(jax.random.fold_in(key, 6), dim), (shards_of,), jnp.float32, low / len(split), high / len(split))
        return jnp.repeat(jnp.exp(heights), extent[dim] // shards_of).reshape((-1,) + (1,) * (len(extent) - dim - 1))

    factor_of = one(*split[0])
    for cut in split[1:]:
        factor_of = factor_of * one(*cut)
    return factor_of


def centred(stream_key, shape, width, limit, cuts=(), kind=jnp.bfloat16):
    gain = level_of(stream_key, shape, cuts, -0.22, 0.18) if cuts else 1.0
    result = jax.random.normal(stream_key, shape, jnp.float32) * width * gain
    return jnp.minimum(jnp.maximum(result, -limit), limit).astype(kind)


def setup_inputs(seed: int = 0) -> dict:
    streams_of = jax.random.split(jax.random.key(seed), 5)
    tracers = centred(streams_of[0], (2, LEV, NY, NX), 1.0, 6.0, ((2, 16), (3, 2)), jnp.float32)
    velocity = centred(streams_of[1], (2, LEV, NY, NX), 0.5, 3.0, ((2, 16), (3, 2)), jnp.float32)
    depth_levels = draw_depth_levels(jax.random.fold_in(streams_of[4], 71), 0)
    vdiff = jnp.clip(jnp.exp(jax.random.uniform(streams_of[3], (LEV - 1,), jnp.float32, math.log(0.05), math.log(0.45))), 0.05, 0.45)
    return {"tracers": tracers, "velocity": velocity, "depth_levels": depth_levels, "vdiff": vdiff}


TIME_STEP = 0.2
MIX_COEF = 0.25
SEA_DIAG = 0.5


def extend_global(fields, fold_sign):
    north_row = fields[:, -1, ::-1] * fold_sign[:, None]
    south_row = jnp.zeros_like(fields[:, :1, :])
    grown = jnp.concatenate([south_row, fields, north_row[:, None, :]], 1)
    return jnp.concatenate([grown[:, :, -1:], grown, grown[:, :, :1]], 2)


def tracer_step(tracer, velocity, depth_pad, vdiff):
    count = tracer.shape[1]
    levels = jnp.arange(count, dtype=jnp.float32)[:, None, None]
    wet_mask = (levels < depth_pad[None]).astype(jnp.float32)
    east_vel = velocity[0]
    north_vel = velocity[1]
    row_set = tracer[:, :, 1:-1, :]
    wet_rows = wet_mask[:, 1:-1, :]
    east_rows = east_vel[:, 1:-1, :]
    east_open = wet_rows[:, :, :-1] * wet_rows[:, :, 1:]
    east_face = 0.5 * (east_rows[:, :, :-1] + east_rows[:, :, 1:])
    east_flux = east_open * (east_face * 0.5 * (row_set[..., :-1] + row_set[..., 1:]) - MIX_COEF * (row_set[..., 1:] - row_set[..., :-1]))
    col_set = tracer[:, :, :, 1:-1]
    wet_cols = wet_mask[:, :, 1:-1]
    north_cols = north_vel[:, :, 1:-1]
    north_open = wet_cols[:, :-1, :] * wet_cols[:, 1:, :]
    north_face = 0.5 * (north_cols[:, :-1, :] + north_cols[:, 1:, :])
    north_flux = north_open * (north_face * 0.5 * (col_set[:, :, :-1, :] + col_set[:, :, 1:, :]) - MIX_COEF * (col_set[:, :, 1:, :] - col_set[:, :, :-1, :]))
    centre = tracer[:, :, 1:-1, 1:-1]
    wet_centre = wet_mask[:, 1:-1, 1:-1]
    vert_open = wet_centre[:-1] * wet_centre[1:]
    vert_flux = vdiff[:, None, None] * vert_open * (centre[:, 1:] - centre[:, :-1])
    border = jnp.zeros_like(centre[:, :1])
    vert_flux = jnp.concatenate([border, vert_flux, border], 1)
    tendency = (vert_flux[:, 1:] - vert_flux[:, :-1]) - (east_flux[..., 1:] - east_flux[..., :-1]) - (north_flux[:, :, 1:, :] - north_flux[:, :, :-1, :])
    return wet_centre * (centre + TIME_STEP * tendency)


def column_forcing(velocity, depth_pad):
    count = velocity.shape[1]
    levels = jnp.arange(count, dtype=jnp.float32)[:, None, None]
    wet_mask = (levels < depth_pad[None]).astype(jnp.float32)
    east_sum = jnp.sum(wet_mask * velocity[0], 0)
    north_sum = jnp.sum(wet_mask * velocity[1], 0)
    ocean_mask = (depth_pad[1:-1, 1:-1] > 0).astype(jnp.float32)
    return ocean_mask * (0.5 * (east_sum[1:-1, 2:] - east_sum[1:-1, :-2]) + 0.5 * (north_sum[2:, 1:-1] - north_sum[:-2, 1:-1]))


def sea_operator(field_pad, depth_pad, count):
    centre = field_pad[1:-1, 1:-1]
    depth_c = depth_pad[1:-1, 1:-1]
    ocean_mask = (depth_c > 0).astype(jnp.float32)
    total = SEA_DIAG * centre
    for rows_at, cols_at in ((slice(1, -1), slice(2, None)), (slice(1, -1), slice(None, -2)), (slice(2, None), slice(1, -1)), (slice(None, -2), slice(1, -1))):
        weight = jnp.minimum(depth_c, depth_pad[rows_at, cols_at]) / count
        total = total + weight * (centre - field_pad[rows_at, cols_at])
    return ocean_mask * total + (1.0 - ocean_mask) * centre


def reference(tracers, velocity, depth_levels, vdiff):
    count = tracers.shape[1]
    height, breadth = depth_levels.shape
    fields = jnp.concatenate([tracers.reshape(2 * count, height, breadth), velocity.reshape(2 * count, height, breadth), depth_levels.astype(jnp.float32)[None]], 0)
    fold_sign = jnp.concatenate([jnp.ones((2 * count,), jnp.float32), -jnp.ones((2 * count,), jnp.float32), jnp.ones((1,), jnp.float32)])
    padded = extend_global(fields, fold_sign)
    tracer_pad = padded[:2 * count].reshape(2, count, height + 2, breadth + 2)
    velocity_pad = padded[2 * count:4 * count].reshape(2, count, height + 2, breadth + 2)
    depth_pad = padded[4 * count]
    new_tracers = tracer_step(tracer_pad, velocity_pad, depth_pad, vdiff)
    forcing = column_forcing(velocity_pad, depth_pad)

    def apply_op(field):
        grown = extend_global(field[None], jnp.ones((1,), jnp.float32))[0]
        return sea_operator(grown, depth_pad, count)

    surface = jnp.zeros_like(forcing)
    residual = forcing
    applied = apply_op(residual)
    norm_now = jnp.sum(residual * residual)
    product = jnp.sum(residual * applied)
    step_len = norm_now / product
    direction, along = residual, applied
    for sweep in range(ITERS):
        surface = surface + step_len * direction
        residual = residual - step_len * along
        if sweep + 1 < ITERS:
            applied = apply_op(residual)
            norm_next = jnp.sum(residual * residual)
            product = jnp.sum(residual * applied)
            beta_ratio = norm_next / norm_now
            step_len = norm_next / (product - beta_ratio * norm_next / step_len)
            direction = residual + beta_ratio * direction
            along = applied + beta_ratio * along
            norm_now = norm_next
    return new_tracers, surface, residual
```

```python
import functools

import jax
import jax.numpy as jnp
from jax import lax
from jax.experimental import pallas as pl
from jax.experimental.pallas import tpu as pltpu
from jax.sharding import PartitionSpec as P

ITERS = 3


TIME_STEP = 0.2
MIX_COEF = 0.25
SEA_DIAG = 0.5

AXES = ("blk", "grp")
GATHER_CELLS = 1 << 17


def swapped(value, axis, stride):
    return lax.ppermute(value, axis, [(i, i ^ 1 << stride) for i in range(lax.axis_size(axis))])


def padded_2(cells, sides, width, closed):
    for axis, dim in sides:
        count = lax.axis_size(axis)
        ends = count if closed else count - 1
        head = lax.slice_in_dim(cells, 0, width, axis=dim)
        tail = lax.slice_in_dim(cells, cells.shape[dim] - width, cells.shape[dim], axis=dim)
        cells = jnp.concatenate(
            [
                lax.ppermute(tail, axis, [(i, (i + 1) % count) for i in range(ends)]),
                cells,
                lax.ppermute(head, axis, [((i + 1) % count, i) for i in range(ends)]),
            ],
            axis=dim,
        )
    return cells


def tracer_step(tracer, velocity, depth_pad, vdiff):
    count = tracer.shape[1]
    levels = jnp.arange(count, dtype=jnp.float32)[:, None, None]
    wet_mask = (levels < depth_pad[None]).astype(jnp.float32)
    east_vel = velocity[0]
    north_vel = velocity[1]
    row_set = tracer[:, :, 1:-1, :]
    wet_rows = wet_mask[:, 1:-1, :]
    east_rows = east_vel[:, 1:-1, :]
    east_open = wet_rows[:, :, :-1] * wet_rows[:, :, 1:]
    east_face = 0.5 * (east_rows[:, :, :-1] + east_rows[:, :, 1:])
    east_flux = east_open * (
        east_face * 0.5 * (row_set[..., :-1] + row_set[..., 1:])
        - MIX_COEF * (row_set[..., 1:] - row_set[..., :-1])
    )
    col_set = tracer[:, :, :, 1:-1]
    wet_cols = wet_mask[:, :, 1:-1]
    north_cols = north_vel[:, :, 1:-1]
    north_open = wet_cols[:, :-1, :] * wet_cols[:, 1:, :]
    north_face = 0.5 * (north_cols[:, :-1, :] + north_cols[:, 1:, :])
    north_flux = north_open * (
        north_face * 0.5 * (col_set[:, :, :-1, :] + col_set[:, :, 1:, :])
        - MIX_COEF * (col_set[:, :, 1:, :] - col_set[:, :, :-1, :])
    )
    centre = tracer[:, :, 1:-1, 1:-1]
    wet_centre = wet_mask[:, 1:-1, 1:-1]
    vert_open = wet_centre[:-1] * wet_centre[1:]
    vert_flux = vdiff[:, None, None] * vert_open * (centre[:, 1:] - centre[:, :-1])
    border = jnp.zeros_like(centre[:, :1])
    vert_flux = jnp.concatenate([border, vert_flux, border], 1)
    tendency = (
        vert_flux[:, 1:]
        - vert_flux[:, :-1]
        - (east_flux[..., 1:] - east_flux[..., :-1])
        - (north_flux[:, :, 1:, :] - north_flux[:, :, :-1, :])
    )
    return wet_centre * (centre + TIME_STEP * tendency)


def column_forcing(velocity, depth_pad):
    count = velocity.shape[1]
    levels = jnp.arange(count, dtype=jnp.float32)[:, None, None]
    wet_mask = (levels < depth_pad[None]).astype(jnp.float32)
    east_sum = jnp.sum(wet_mask * velocity[0], 0)
    north_sum = jnp.sum(wet_mask * velocity[1], 0)
    ocean_mask = (depth_pad[1:-1, 1:-1] > 0).astype(jnp.float32)
    return ocean_mask * (
        0.5 * (east_sum[1:-1, 2:] - east_sum[1:-1, :-2])
        + 0.5 * (north_sum[2:, 1:-1] - north_sum[:-2, 1:-1])
    )


def sea_operator(field_pad, depth_pad, count):
    centre = field_pad[1:-1, 1:-1]
    depth_c = depth_pad[1:-1, 1:-1]
    ocean_mask = (depth_c > 0).astype(jnp.float32)
    total = SEA_DIAG * centre
    for rows_at, cols_at in (
        (slice(1, -1), slice(2, None)),
        (slice(1, -1), slice(None, -2)),
        (slice(2, None), slice(1, -1)),
        (slice(None, -2), slice(1, -1)),
    ):
        weight = jnp.minimum(depth_c, depth_pad[rows_at, cols_at]) / count
        total = total + weight * (centre - field_pad[rows_at, cols_at])
    return ocean_mask * total + (1.0 - ocean_mask) * centre


def extend(fields, fold_sign):
    top_row = fields[:, -1, :]
    partner = top_row
    for bit_index in range(lax.axis_size("grp").bit_length() - 1):
        partner = swapped(partner, "grp", bit_index)
    mirror = partner[:, ::-1]
    northmost = lax.axis_index("blk") == lax.axis_size("blk") - 1
    row_halo = padded_2(fields, (("blk", 1),), 1, False)
    north_row = jnp.where(northmost, mirror * fold_sign[:, None], row_halo[:, -1, :])
    grown = jnp.concatenate([row_halo[:, :-1, :], north_row[:, None, :]], 1)
    return padded_2(grown, (("grp", 2),), 1, True)


def two_sums(residual, applied):
    return lax.psum((jnp.sum(residual * residual), jnp.sum(residual * applied)), AXES)


def wide_shards(tracers, velocity, depth_levels, vdiff):
    count = tracers.shape[1]
    height, breadth = depth_levels.shape
    fields = jnp.concatenate(
        [
            tracers.reshape(2 * count, height, breadth),
            velocity.reshape(2 * count, height, breadth),
            depth_levels.astype(jnp.float32)[None],
        ],
        0,
    )
    fold_sign = jnp.concatenate(
        [
            jnp.ones((2 * count,), jnp.float32),
            -jnp.ones((2 * count,), jnp.float32),
            jnp.ones((1,), jnp.float32),
        ]
    )
    padded = extend(fields, fold_sign)
    tracer_pad = padded[: 2 * count].reshape(2, count, height + 2, breadth + 2)
    velocity_pad = padded[2 * count : 4 * count].reshape(2, count, height + 2, breadth + 2)
    depth_pad = padded[4 * count]
    new_tracers = tracer_step(tracer_pad, velocity_pad, depth_pad, vdiff)
    forcing = column_forcing(velocity_pad, depth_pad)

    def apply_op(field):
        grown = extend(field[None], jnp.ones((1,), jnp.float32))[0]
        return sea_operator(grown, depth_pad, count)

    surface = jnp.zeros_like(forcing)
    residual = forcing
    applied = apply_op(residual)
    norm_now, product = two_sums(residual, applied)
    step_len = norm_now / product
    direction, along = (residual, applied)
    for sweep in range(ITERS):
        surface = surface + step_len * direction
        residual = residual - step_len * along
        if sweep + 1 < ITERS:
            applied = apply_op(residual)
            norm_next, product = two_sums(residual, applied)
            beta_ratio = norm_next / norm_now
            step_len = norm_next / (product - beta_ratio * norm_next / step_len)
            direction = residual + beta_ratio * direction
            along = applied + beta_ratio * along
            norm_now = norm_next
    return (new_tracers, surface, residual)


SUB, LANE = 8, 128


def tile_iota(dim):
    return lax.broadcasted_iota(jnp.int32, (SUB, LANE), dim)


def reversed_lanes(value):
    index = LANE - 1 - lax.broadcasted_iota(jnp.int32, value.shape, 1)
    return jnp.take_along_axis(value, index, axis=1)


def pack_kernel(count, tracers_ref, velocity_ref, depth_ref, sums_ref, low_ref, high_ref, edge_ref):
    depth = depth_ref[...]
    east = jnp.zeros((SUB, LANE), jnp.float32)
    north = jnp.zeros((SUB, LANE), jnp.float32)
    for level in range(count):
        wet = depth > level
        east += jnp.where(wet, velocity_ref[pl.ds(level * SUB, SUB), :], 0.0)
        north += jnp.where(wet, velocity_ref[pl.ds((count + level) * SUB, SUB), :], 0.0)
    depth_f = depth.astype(jnp.float32)
    sums_ref[0:SUB, :] = east
    sums_ref[SUB : 2 * SUB, :] = north
    sums_ref[2 * SUB : 3 * SUB, :] = depth_f
    for out_ref, row in ((low_ref, 0), (high_ref, SUB - 1)):
        out_ref[0 : 2 * count, :] = tracers_ref[pl.ds(row, 2 * count, stride=SUB), :]
        out_ref[2 * count : 3 * count, :] = velocity_ref[pl.ds(count * SUB + row, count, stride=SUB), :]
        out_ref[3 * count : 3 * count + SUB, :] = jnp.broadcast_to(depth_f[row : row + 1, :], (SUB, LANE))
    lane = tile_iota(1)
    west_pack = jnp.zeros((SUB, LANE), jnp.float32)
    east_pack = jnp.zeros((SUB, LANE), jnp.float32)
    for field in range(3 * count + 1):
        if field < 2 * count:
            tile = tracers_ref[pl.ds(field * SUB, SUB), :]
        elif field < 3 * count:
            tile = velocity_ref[pl.ds((field - 2 * count) * SUB, SUB), :]
        else:
            tile = depth_f
        west_pack = jnp.where(lane == field, pltpu.roll(tile, field, 1), west_pack)
        east_pack = jnp.where(lane == field, pltpu.roll(tile, field + 1, 1), east_pack)
    edge_ref[0:SUB, :] = west_pack
    edge_ref[SUB : 2 * SUB, :] = east_pack


def tracer_kernel(
    count, blocks, place_ref, vdiff_ref, tracers_ref, velocity_ref, depth_ref, core_ref, far_ref, edge_ref, out_ref
):
    blk = place_ref[0] // 2
    odd = (blk % 2) == 1
    fold = blk == blocks - 1
    lane, sub = tile_iota(1), tile_iota(0)
    rows = core_ref.shape[0]
    near = core_ref[...]
    far = far_ref[...]
    row_id = lax.broadcasted_iota(jnp.int32, (rows, LANE), 0)
    sign = jnp.where((row_id >= 2 * count) & (row_id < 3 * count), -1.0, 1.0)
    far_north = jnp.where(fold, reversed_lanes(far) * sign, far)
    north_rows = jnp.where(odd, far_north, near)
    south_rows = jnp.where(odd, near, far)
    edge_base = edge_ref.shape[0] - 2 * SUB
    east_cols = edge_ref[edge_base : edge_base + SUB, :]
    west_cols = edge_ref[edge_base + SUB : edge_base + 2 * SUB, :]

    def spread(packed, field, at):
        return pltpu.roll(packed, (at - field) % LANE, 1)

    def east_of(tile, field):
        return jnp.where(lane == LANE - 1, spread(east_cols, field, LANE - 1), pltpu.roll(tile, LANE - 1, 1))

    def west_of(tile, field):
        return jnp.where(lane == 0, spread(west_cols, field, 0), pltpu.roll(tile, 1, 1))

    def north_of(tile, field):
        ghost = jnp.broadcast_to(north_rows[field : field + 1, :], (SUB, LANE))
        return jnp.where(sub == SUB - 1, ghost, pltpu.roll(tile, SUB - 1, 0))

    def south_of(tile, field):
        ghost = jnp.broadcast_to(south_rows[field : field + 1, :], (SUB, LANE))
        return jnp.where(sub == 0, ghost, pltpu.roll(tile, 1, 0))

    depth = depth_ref[...].astype(jnp.float32)
    at = 3 * count
    open_east = jnp.minimum(depth, east_of(depth, at))
    open_west = jnp.minimum(depth, west_of(depth, at))
    open_north = jnp.minimum(depth, north_of(depth, at))
    open_south = jnp.minimum(depth, south_of(depth, at))

    def flux(here, there, speed):
        return speed * (there + here) - MIX_COEF * (there - here)

    below = [None, None]
    for level in range(count):
        u = velocity_ref[pl.ds(level * SUB, SUB), :]
        v = velocity_ref[pl.ds((count + level) * SUB, SUB), :]
        k = float(level)
        east_speed = 0.25 * (u + east_of(u, 2 * count + level))
        west_speed = 0.25 * (u + west_of(u, 2 * count + level))
        north_speed = 0.25 * (v + north_of(v, 2 * count + level))
        south_speed = 0.25 * (v + south_of(v, 2 * count + level))
        for which in range(2):
            field = which * count + level
            here = tracers_ref[pl.ds(field * SUB, SUB), :]
            out = jnp.where(open_east > k, flux(here, east_of(here, field), east_speed), 0.0)
            out -= jnp.where(open_west > k, flux(west_of(here, field), here, west_speed), 0.0)
            out += jnp.where(open_north > k, flux(here, north_of(here, field), north_speed), 0.0)
            out -= jnp.where(open_south > k, flux(south_of(here, field), here, south_speed), 0.0)
            tendency = -out
            if level + 1 < count:
                under = tracers_ref[pl.ds((field + 1) * SUB, SUB), :]
                vertical = jnp.where(depth > k + 1.0, vdiff_ref[level] * (under - here), 0.0)
                tendency += vertical
            else:
                vertical = None
            if below[which] is not None:
                tendency -= below[which]
            below[which] = vertical
            out_ref[pl.ds(field * SUB, SUB), :] = jnp.where(depth > k, here + TIME_STEP * tendency, 0.0)


def solve_kernel(count, blocks, order, place_ref, own_ref, other_ref, surface_ref, residual_ref, fields, scratch):
    me = place_ref[0]
    core = (me // 2) % 2
    height = blocks * SUB

    for blk in range(blocks):
        for grp in range(2):
            apart = (blk * 2 + grp) ^ me
            slot = 0
            for bit, at in enumerate(order):
                slot = slot + ((apart >> at) & 1) * (1 << bit)
            mine = core == (blk % 2)
            for part in range(3):
                value = jnp.where(
                    mine,
                    own_ref[slot, part * SUB : (part + 1) * SUB, :],
                    other_ref[slot, part * SUB : (part + 1) * SUB, :],
                )
                fields[part, grp, blk * SUB : (blk + 1) * SUB, :] = value

    shape = (height, LANE)
    lane = lax.broadcasted_iota(jnp.int32, shape, 1)
    sub = tile_iota(0)

    def east_of(pair):
        low, high = (pltpu.roll(half, LANE - 1, 1) for half in pair)
        return jnp.where(lane == LANE - 1, high, low), jnp.where(lane == LANE - 1, low, high)

    def west_of(pair):
        low, high = (pltpu.roll(half, 1, 1) for half in pair)
        return jnp.where(lane == 0, high, low), jnp.where(lane == 0, low, high)

    def north_of(pair, sign=1.0):
        out = []
        for half, mirror in zip(pair, pair[::-1]):
            moved = pltpu.roll(half, height - 1, 0)
            ghost = reversed_lanes(mirror[height - SUB :, :]) * sign
            top = jnp.where(sub == SUB - 1, ghost, moved[height - SUB :, :])
            out.append(jnp.concatenate([moved[: height - SUB, :], top], 0))
        return tuple(out)

    def south_of(pair):
        out = []
        for half in pair:
            moved = pltpu.roll(half, 1, 0)
            bottom = jnp.where(sub == 0, 0.0, moved[:SUB, :])
            out.append(jnp.concatenate([bottom, moved[SUB:, :]], 0))
        return tuple(out)

    u = (fields[0, 0], fields[0, 1])
    v = (fields[1, 0], fields[1, 1])
    depth = (fields[2, 0], fields[2, 1])
    weight_east = tuple(jnp.minimum(a, b) * (1.0 / count) for a, b in zip(depth, east_of(depth)))
    weight_north = tuple(jnp.minimum(a, b) * (1.0 / count) for a, b in zip(depth, north_of(depth)))
    diagonal = tuple(jnp.where(d > 0.0, SEA_DIAG, 1.0) for d in depth)

    ue, uw, vn, vs = east_of(u), west_of(u), north_of(v, -1.0), south_of(v)
    forcing = tuple(
        jnp.where(depth[i] > 0.0, 0.5 * (ue[i] - uw[i]) + 0.5 * (vn[i] - vs[i]), 0.0) for i in range(2)
    )

    def apply_op(x):
        xe, xn = east_of(x), north_of(x)
        flux_e = tuple(weight_east[i] * (xe[i] - x[i]) for i in range(2))
        flux_n = tuple(weight_north[i] * (xn[i] - x[i]) for i in range(2))
        fw, fs = west_of(flux_e), south_of(flux_n)
        return tuple(diagonal[i] * x[i] - (flux_e[i] - fw[i]) - (flux_n[i] - fs[i]) for i in range(2))

    def total(a, b):
        part = a[0] * b[0] + a[1] * b[1]
        return jnp.sum(jnp.sum(part.reshape(blocks, SUB, LANE), 0), keepdims=True)

    grp = me % 2
    mine = pl.ds(pl.multiple_of((me // 2) * SUB, SUB), SUB)

    def own(pair):
        scratch[0] = pair[0]
        scratch[1] = pair[1]
        return jnp.where(grp == 0, scratch[0, mine, :], scratch[1, mine, :])

    residual = forcing
    applied = apply_op(residual)
    norm_now, product = total(residual, residual), total(residual, applied)
    step_len = norm_now / product
    along = applied
    own_residual = own(residual)
    own_along = own(applied)
    own_direction = own_residual
    own_surface = jnp.zeros((SUB, LANE), jnp.float32)
    for sweep in range(ITERS):
        own_surface = own_surface + step_len * own_direction
        own_residual = own_residual - step_len * own_along
        if sweep + 1 < ITERS:
            residual = tuple(residual[i] - step_len * along[i] for i in range(2))
            applied = apply_op(residual)
            norm_next, product = total(residual, residual), total(residual, applied)
            beta_ratio = norm_next / norm_now
            step_len = norm_next / (product - beta_ratio * norm_next / step_len)
            own_direction = own_residual + beta_ratio * own_direction
            own_along = own(applied) + beta_ratio * own_along
            if sweep + 2 < ITERS:
                along = tuple(applied[i] + beta_ratio * along[i] for i in range(2))
            norm_now = norm_next
    surface_ref[...] = own_surface
    residual_ref[...] = own_residual


VMEM_SPEC = pl.BlockSpec(memory_space=pltpu.VMEM)
SMEM_SPEC = pl.BlockSpec(memory_space=pltpu.SMEM)


def tile_shape(rows):
    return jax.ShapeDtypeStruct((rows, LANE), jnp.float32)


def small_shards(tracers, velocity, depth_levels, vdiff):
    count = tracers.shape[1]
    blocks = lax.axis_size("blk")
    devices = blocks * 2
    tracer_rows = tracers.reshape(2 * count * SUB, LANE)
    velocity_rows = velocity.reshape(2 * count * SUB, LANE)
    place = (lax.axis_index("blk") * 2 + lax.axis_index("grp")).astype(jnp.int32)
    odd = lax.axis_index("blk") % 2 == 1

    halo_rows = 3 * count + SUB
    sums, low, high, edges = pl.pallas_call(
        functools.partial(pack_kernel, count),
        out_shape=[tile_shape(3 * SUB), tile_shape(halo_rows), tile_shape(halo_rows), tile_shape(2 * SUB)],
        in_specs=[VMEM_SPEC] * 3,
        out_specs=[VMEM_SPEC] * 4,
        name="pack",
    )(tracer_rows, velocity_rows, depth_levels)

    near = lax.ppermute(jnp.where(odd, low, high), AXES, [(i, i ^ 2) for i in range(devices)])
    far_pairs = []
    for blk in range(1, blocks, 2):
        for grp in range(2):
            here = blk * 2 + grp
            there = here ^ 1 if blk == blocks - 1 else here + 2
            far_pairs.append((here, there))
            if blk < blocks - 1:
                far_pairs.append((there, here))
    far = lax.ppermute(jnp.where(odd, high, low), AXES, far_pairs)

    top = devices.bit_length() - 1
    order = [bit for bit in range(top - 1, 2, -1)] + [0, 2]
    gathered = sums
    edge_pack = None
    for bit in order:
        pairs = [(i, i ^ 1 << bit) for i in range(devices)]
        if bit == 0:
            both = lax.ppermute(jnp.concatenate([gathered, edges], 0), AXES, pairs)
            edge_pack = both
            gathered = jnp.concatenate([gathered, both[: gathered.shape[0]]], 0)
        else:
            gathered = jnp.concatenate([gathered, lax.ppermute(gathered, AXES, pairs)], 0)
    other = lax.ppermute(gathered, AXES, [(i, i ^ 2) for i in range(devices)])
    slots = devices // 2

    place_arr = place.reshape(1)
    new_rows = pl.pallas_call(
        functools.partial(tracer_kernel, count, blocks),
        out_shape=tile_shape(2 * count * SUB),
        in_specs=[SMEM_SPEC, SMEM_SPEC] + [VMEM_SPEC] * 6,
        out_specs=VMEM_SPEC,
        name="tracer",
    )(place_arr, vdiff, tracer_rows, velocity_rows, depth_levels, near, far, edge_pack)

    surface, residual = pl.pallas_call(
        functools.partial(solve_kernel, count, blocks, tuple(order)),
        out_shape=[tile_shape(SUB), tile_shape(SUB)],
        in_specs=[SMEM_SPEC] + [VMEM_SPEC] * 2,
        out_specs=[VMEM_SPEC] * 2,
        scratch_shapes=[
            pltpu.VMEM((3, 2, blocks * SUB, LANE), jnp.float32),
            pltpu.VMEM((2, blocks * SUB, LANE), jnp.float32),
        ],
        name="solve",
    )(place_arr, gathered.reshape(slots, 3 * SUB, LANE), other.reshape(slots, 3 * SUB, LANE))
    return new_rows.reshape(tracers.shape), surface, residual


def shards(tracers, velocity, depth_levels, vdiff):
    blocks, groups = lax.axis_size("blk"), lax.axis_size("grp")
    height, breadth = depth_levels.shape
    tiled = (height, breadth) == (SUB, LANE) and groups == 2 and blocks >= 4 and blocks & (blocks - 1) == 0
    if tiled and 3 * tracers.shape[1] < LANE and blocks * groups * SUB * LANE <= GATHER_CELLS:
        return small_shards(tracers, velocity, depth_levels, vdiff)
    return wide_shards(tracers, velocity, depth_levels, vdiff)


def solution(mesh):
    return jax.shard_map(
        shards,
        mesh=mesh,
        in_specs=(P(None, None, "blk", "grp"), P(None, None, "blk", "grp"), P("blk", "grp"), P()),
        out_specs=(P(None, None, "blk", "grp"), P("blk", "grp"), P("blk", "grp")),
        check_vma=False,
    )
```

```python
import functools

import jax
import jax.numpy as jnp
from jax import lax
from jax.experimental import pallas as pl
from jax.experimental.pallas import tpu as pltpu
from jax.sharding import PartitionSpec as P


ITERS = 3


TIME_STEP = 0.2
MIX_COEF = 0.25
SEA_DIAG = 0.5

AXES = ("blk", "grp")
GATHER_CELLS = 1 << 17


def swapped(value, axis, stride):
    return lax.ppermute(value, axis, [(i, i ^ 1 << stride) for i in range(lax.axis_size(axis))])


def padded_2(cells, sides, width, closed):
    for axis, dim in sides:
        count = lax.axis_size(axis)
        ends = count if closed else count - 1
        head = lax.slice_in_dim(cells, 0, width, axis=dim)
        tail = lax.slice_in_dim(cells, cells.shape[dim] - width, cells.shape[dim], axis=dim)
        cells = jnp.concatenate(
            [
                lax.ppermute(tail, axis, [(i, (i + 1) % count) for i in range(ends)]),
                cells,
                lax.ppermute(head, axis, [((i + 1) % count, i) for i in range(ends)]),
            ],
            axis=dim,
        )
    return cells


def tracer_step(tracer, velocity, depth_pad, vdiff):
    count = tracer.shape[1]
    levels = jnp.arange(count, dtype=jnp.float32)[:, None, None]
    wet_mask = (levels < depth_pad[None]).astype(jnp.float32)
    east_vel = velocity[0]
    north_vel = velocity[1]
    row_set = tracer[:, :, 1:-1, :]
    wet_rows = wet_mask[:, 1:-1, :]
    east_rows = east_vel[:, 1:-1, :]
    east_open = wet_rows[:, :, :-1] * wet_rows[:, :, 1:]
    east_face = 0.5 * (east_rows[:, :, :-1] + east_rows[:, :, 1:])
    east_flux = east_open * (
        east_face * 0.5 * (row_set[..., :-1] + row_set[..., 1:])
        - MIX_COEF * (row_set[..., 1:] - row_set[..., :-1])
    )
    col_set = tracer[:, :, :, 1:-1]
    wet_cols = wet_mask[:, :, 1:-1]
    north_cols = north_vel[:, :, 1:-1]
    north_open = wet_cols[:, :-1, :] * wet_cols[:, 1:, :]
    north_face = 0.5 * (north_cols[:, :-1, :] + north_cols[:, 1:, :])
    north_flux = north_open * (
        north_face * 0.5 * (col_set[:, :, :-1, :] + col_set[:, :, 1:, :])
        - MIX_COEF * (col_set[:, :, 1:, :] - col_set[:, :, :-1, :])
    )
    centre = tracer[:, :, 1:-1, 1:-1]
    wet_centre = wet_mask[:, 1:-1, 1:-1]
    vert_open = wet_centre[:-1] * wet_centre[1:]
    vert_flux = vdiff[:, None, None] * vert_open * (centre[:, 1:] - centre[:, :-1])
    border = jnp.zeros_like(centre[:, :1])
    vert_flux = jnp.concatenate([border, vert_flux, border], 1)
    tendency = (
        vert_flux[:, 1:]
        - vert_flux[:, :-1]
        - (east_flux[..., 1:] - east_flux[..., :-1])
        - (north_flux[:, :, 1:, :] - north_flux[:, :, :-1, :])
    )
    return wet_centre * (centre + TIME_STEP * tendency)


def column_forcing(velocity, depth_pad):
    count = velocity.shape[1]
    levels = jnp.arange(count, dtype=jnp.float32)[:, None, None]
    wet_mask = (levels < depth_pad[None]).astype(jnp.float32)
    east_sum = jnp.sum(wet_mask * velocity[0], 0)
    north_sum = jnp.sum(wet_mask * velocity[1], 0)
    ocean_mask = (depth_pad[1:-1, 1:-1] > 0).astype(jnp.float32)
    return ocean_mask * (
        0.5 * (east_sum[1:-1, 2:] - east_sum[1:-1, :-2])
        + 0.5 * (north_sum[2:, 1:-1] - north_sum[:-2, 1:-1])
    )


def sea_operator(field_pad, depth_pad, count):
    centre = field_pad[1:-1, 1:-1]
    depth_c = depth_pad[1:-1, 1:-1]
    ocean_mask = (depth_c > 0).astype(jnp.float32)
    total = SEA_DIAG * centre
    for rows_at, cols_at in (
        (slice(1, -1), slice(2, None)),
        (slice(1, -1), slice(None, -2)),
        (slice(2, None), slice(1, -1)),
        (slice(None, -2), slice(1, -1)),
    ):
        weight = jnp.minimum(depth_c, depth_pad[rows_at, cols_at]) / count
        total = total + weight * (centre - field_pad[rows_at, cols_at])
    return ocean_mask * total + (1.0 - ocean_mask) * centre


def extend(fields, fold_sign):
    top_row = fields[:, -1, :]
    partner = top_row
    for bit_index in range(lax.axis_size("grp").bit_length() - 1):
        partner = swapped(partner, "grp", bit_index)
    mirror = partner[:, ::-1]
    northmost = lax.axis_index("blk") == lax.axis_size("blk") - 1
    row_halo = padded_2(fields, (("blk", 1),), 1, False)
    north_row = jnp.where(northmost, mirror * fold_sign[:, None], row_halo[:, -1, :])
    grown = jnp.concatenate([row_halo[:, :-1, :], north_row[:, None, :]], 1)
    return padded_2(grown, (("grp", 2),), 1, True)


def two_sums(residual, applied):
    return lax.psum((jnp.sum(residual * residual), jnp.sum(residual * applied)), AXES)


def wide_shards(tracers, velocity, depth_levels, vdiff):
    count = tracers.shape[1]
    height, breadth = depth_levels.shape
    fields = jnp.concatenate(
        [
            tracers.reshape(2 * count, height, breadth),
            velocity.reshape(2 * count, height, breadth),
            depth_levels.astype(jnp.float32)[None],
        ],
        0,
    )
    fold_sign = jnp.concatenate(
        [
            jnp.ones((2 * count,), jnp.float32),
            -jnp.ones((2 * count,), jnp.float32),
            jnp.ones((1,), jnp.float32),
        ]
    )
    padded = extend(fields, fold_sign)
    tracer_pad = padded[: 2 * count].reshape(2, count, height + 2, breadth + 2)
    velocity_pad = padded[2 * count : 4 * count].reshape(2, count, height + 2, breadth + 2)
    depth_pad = padded[4 * count]
    new_tracers = tracer_step(tracer_pad, velocity_pad, depth_pad, vdiff)
    forcing = column_forcing(velocity_pad, depth_pad)

    def apply_op(field):
        grown = extend(field[None], jnp.ones((1,), jnp.float32))[0]
        return sea_operator(grown, depth_pad, count)

    surface = jnp.zeros_like(forcing)
    residual = forcing
    applied = apply_op(residual)
    norm_now, product = two_sums(residual, applied)
    step_len = norm_now / product
    direction, along = (residual, applied)
    for sweep in range(ITERS):
        surface = surface + step_len * direction
        residual = residual - step_len * along
        if sweep + 1 < ITERS:
            applied = apply_op(residual)
            norm_next, product = two_sums(residual, applied)
            beta_ratio = norm_next / norm_now
            step_len = norm_next / (product - beta_ratio * norm_next / step_len)
            direction = residual + beta_ratio * direction
            along = applied + beta_ratio * along
            norm_now = norm_next
    return (new_tracers, surface, residual)


SUB, LANE = 8, 128


def tile_iota(dim):
    return lax.broadcasted_iota(jnp.int32, (SUB, LANE), dim)


def reversed_lanes(value):
    index = LANE - 1 - lax.broadcasted_iota(jnp.int32, value.shape, 1)
    return jnp.take_along_axis(value, index, axis=1)


def pack_kernel(
    count, tracers_hbm, velocity_hbm, depth_hbm, sums_ref, near_ref, far_ref, tracers_ref, velocity_ref, depth_ref, sems
):
    copies = [
        pltpu.make_async_copy(src, dst, sems.at[at])
        for at, (src, dst) in enumerate(
            ((depth_hbm, depth_ref), (velocity_hbm, velocity_ref), (tracers_hbm, tracers_ref))
        )
    ]
    for copy in copies:
        copy.start()
    odd = lax.axis_index("blk") % 2 == 1
    copies[0].wait()
    copies[1].wait()
    depth = depth_ref[...]
    east = jnp.zeros((SUB, LANE), jnp.float32)
    north = jnp.zeros((SUB, LANE), jnp.float32)
    for level in range(count):
        wet = depth > level
        east += jnp.where(wet, velocity_ref[pl.ds(level * SUB, SUB), :], 0.0)
        north += jnp.where(wet, velocity_ref[pl.ds((count + level) * SUB, SUB), :], 0.0)
    depth_f = depth.astype(jnp.float32)
    sums_ref[0:SUB, :] = east
    sums_ref[SUB : 2 * SUB, :] = north
    sums_ref[2 * SUB : 3 * SUB, :] = depth_f
    copies[2].wait()

    def both(ref, first, rows):
        low = ref[pl.ds(first, rows, stride=SUB), :]
        high = ref[pl.ds(first + SUB - 1, rows, stride=SUB), :]
        return jnp.where(odd, low, high), jnp.where(odd, high, low)

    depth_low = jnp.broadcast_to(depth_f[0:1, :], (SUB, LANE))
    depth_high = jnp.broadcast_to(depth_f[SUB - 1 : SUB, :], (SUB, LANE))
    parts = (
        both(tracers_ref, 0, 2 * count),
        both(velocity_ref, count * SUB, count),
        (jnp.where(odd, depth_low, depth_high), jnp.where(odd, depth_high, depth_low)),
    )
    at = 0
    for near, far in parts:
        near_ref[at : at + near.shape[0], :] = near
        far_ref[at : at + near.shape[0], :] = far
        at += near.shape[0]
    lane = tile_iota(1)
    west_pack = jnp.zeros((SUB, LANE), jnp.float32)
    east_pack = jnp.zeros((SUB, LANE), jnp.float32)
    for field in range(3 * count + 1):
        if field < 2 * count:
            tile = tracers_ref[pl.ds(field * SUB, SUB), :]
        elif field < 3 * count:
            tile = velocity_ref[pl.ds((field - 2 * count) * SUB, SUB), :]
        else:
            tile = depth_f
        west_pack = jnp.where(lane == field, pltpu.roll(tile, field, 1), west_pack)
        east_pack = jnp.where(lane == field, pltpu.roll(tile, field + 1, 1), east_pack)
    near_ref[at : at + SUB, :] = west_pack
    near_ref[at + SUB : at + 2 * SUB, :] = east_pack


def tracer_kernel(
    count, blocks, vdiff_ref, tracers_ref, velocity_ref, depth_ref, near_ref, far_ref, edge_ref, out_ref
):
    blk = lax.axis_index("blk")
    odd = blk % 2 == 1
    fold = blk == blocks - 1
    lane, sub = tile_iota(1), tile_iota(0)
    rows = far_ref.shape[0]
    near = near_ref[0:rows, :]
    far = jnp.where(blk == 0, 0.0, far_ref[...])
    row_id = lax.broadcasted_iota(jnp.int32, (rows, LANE), 0)
    sign = jnp.where((row_id >= 2 * count) & (row_id < 3 * count), -1.0, 1.0)
    far_north = jnp.where(fold, reversed_lanes(far) * sign, far)
    north_rows = jnp.where(odd, far_north, near)
    south_rows = jnp.where(odd, near, far)
    edge_base = edge_ref.shape[0] - 2 * SUB
    east_cols = edge_ref[edge_base : edge_base + SUB, :]
    west_cols = edge_ref[edge_base + SUB : edge_base + 2 * SUB, :]

    def spread(packed, field, at):
        return pltpu.roll(packed, (at - field) % LANE, 1)

    def east_of(tile, field):
        return jnp.where(lane == LANE - 1, spread(east_cols, field, LANE - 1), pltpu.roll(tile, LANE - 1, 1))

    def west_of(tile, field):
        return jnp.where(lane == 0, spread(west_cols, field, 0), pltpu.roll(tile, 1, 1))

    def north_of(tile, field):
        ghost = jnp.broadcast_to(north_rows[field : field + 1, :], (SUB, LANE))
        return jnp.where(sub == SUB - 1, ghost, pltpu.roll(tile, SUB - 1, 0))

    def south_of(tile, field):
        ghost = jnp.broadcast_to(south_rows[field : field + 1, :], (SUB, LANE))
        return jnp.where(sub == 0, ghost, pltpu.roll(tile, 1, 0))

    depth = depth_ref[...].astype(jnp.float32)
    at = 3 * count
    open_east = jnp.minimum(depth, east_of(depth, at))
    open_west = jnp.minimum(depth, west_of(depth, at))
    open_north = jnp.minimum(depth, north_of(depth, at))
    open_south = jnp.minimum(depth, south_of(depth, at))

    def flux(here, there, speed):
        return speed * (there + here) - MIX_COEF * (there - here)

    below = [None, None]
    for level in range(count):
        u = velocity_ref[pl.ds(level * SUB, SUB), :]
        v = velocity_ref[pl.ds((count + level) * SUB, SUB), :]
        k = float(level)
        east_speed = 0.25 * (u + east_of(u, 2 * count + level))
        west_speed = 0.25 * (u + west_of(u, 2 * count + level))
        north_speed = 0.25 * (v + north_of(v, 2 * count + level))
        south_speed = 0.25 * (v + south_of(v, 2 * count + level))
        for which in range(2):
            field = which * count + level
            here = tracers_ref[pl.ds(field * SUB, SUB), :]
            out = jnp.where(open_east > k, flux(here, east_of(here, field), east_speed), 0.0)
            out -= jnp.where(open_west > k, flux(west_of(here, field), here, west_speed), 0.0)
            out += jnp.where(open_north > k, flux(here, north_of(here, field), north_speed), 0.0)
            out -= jnp.where(open_south > k, flux(south_of(here, field), here, south_speed), 0.0)
            tendency = -out
            if level + 1 < count:
                under = tracers_ref[pl.ds((field + 1) * SUB, SUB), :]
                vertical = jnp.where(depth > k + 1.0, vdiff_ref[level] * (under - here), 0.0)
                tendency += vertical
            else:
                vertical = None
            if below[which] is not None:
                tendency -= below[which]
            below[which] = vertical
            out_ref[pl.ds(field * SUB, SUB), :] = jnp.where(depth > k, here + TIME_STEP * tendency, 0.0)


def solve_kernel(count, blocks, order, own_ref, other_ref, surface_ref, residual_ref, scratch):
    me = lax.axis_index("blk") * 2 + lax.axis_index("grp")
    height = blocks * SUB

    def slot_of(place):
        return sum(((place >> at) & 1) << bit for bit, at in enumerate(order))

    def core_of(place):
        return sum((place >> at) & 1 for at in (*order, 1)) & 1

    my_slot, my_core = slot_of(me), core_of(me)

    def tile(part, place):
        rows = slice(part * SUB, (part + 1) * SUB)
        slot = slot_of(place) ^ my_slot
        return jnp.where(my_core == core_of(place), own_ref[slot, rows, :], other_ref[slot, rows, :])

    def field(part):
        return tuple(jnp.concatenate([tile(part, blk * 2 + grp) for blk in range(blocks)], 0) for grp in range(2))

    shape = (height, LANE)
    lane = lax.broadcasted_iota(jnp.int32, shape, 1)
    sub = tile_iota(0)

    def east_of(pair):
        low, high = (pltpu.roll(half, LANE - 1, 1) for half in pair)
        return jnp.where(lane == LANE - 1, high, low), jnp.where(lane == LANE - 1, low, high)

    def west_of(pair):
        low, high = (pltpu.roll(half, 1, 1) for half in pair)
        return jnp.where(lane == 0, high, low), jnp.where(lane == 0, low, high)

    def north_of(pair, sign=1.0):
        out = []
        for half, mirror in zip(pair, pair[::-1]):
            moved = pltpu.roll(half, height - 1, 0)
            ghost = reversed_lanes(mirror[height - SUB :, :]) * sign
            top = jnp.where(sub == SUB - 1, ghost, moved[height - SUB :, :])
            out.append(jnp.concatenate([moved[: height - SUB, :], top], 0))
        return tuple(out)

    def south_of(pair):
        out = []
        for half in pair:
            moved = pltpu.roll(half, 1, 0)
            bottom = jnp.where(sub == 0, 0.0, moved[:SUB, :])
            out.append(jnp.concatenate([bottom, moved[SUB:, :]], 0))
        return tuple(out)

    u, v, depth = field(0), field(1), field(2)
    weight_east = tuple(jnp.minimum(a, b) * (1.0 / count) for a, b in zip(depth, east_of(depth)))
    weight_north = tuple(jnp.minimum(a, b) * (1.0 / count) for a, b in zip(depth, north_of(depth)))
    diagonal = tuple(jnp.where(d > 0.0, SEA_DIAG, 1.0) for d in depth)

    ue, uw, vn, vs = east_of(u), west_of(u), north_of(v, -1.0), south_of(v)
    forcing = tuple(
        jnp.where(depth[i] > 0.0, 0.5 * (ue[i] - uw[i]) + 0.5 * (vn[i] - vs[i]), 0.0) for i in range(2)
    )

    def apply_op(x):
        xe, xn = east_of(x), north_of(x)
        flux_e = tuple(weight_east[i] * (xe[i] - x[i]) for i in range(2))
        flux_n = tuple(weight_north[i] * (xn[i] - x[i]) for i in range(2))
        fw, fs = west_of(flux_e), south_of(flux_n)
        return tuple(diagonal[i] * x[i] - (flux_e[i] - fw[i]) - (flux_n[i] - fs[i]) for i in range(2))

    def total(a, b):
        part = a[0] * b[0] + a[1] * b[1]
        return jnp.sum(jnp.sum(part.reshape(blocks, SUB, LANE), 0), keepdims=True)

    grp = me % 2
    mine = pl.ds(pl.multiple_of((me // 2) * SUB, SUB), SUB)

    def own(pair):
        scratch[0] = pair[0]
        scratch[1] = pair[1]
        return jnp.where(grp == 0, scratch[0, mine, :], scratch[1, mine, :])

    residual = forcing
    applied = apply_op(residual)
    norm_now, product = total(residual, residual), total(residual, applied)
    step_len = norm_now / product
    along = applied
    own_residual = own(residual)
    own_along = own(applied)
    own_direction = own_residual
    own_surface = jnp.zeros((SUB, LANE), jnp.float32)
    for sweep in range(ITERS):
        own_surface = own_surface + step_len * own_direction
        own_residual = own_residual - step_len * own_along
        if sweep + 1 < ITERS:
            residual = tuple(residual[i] - step_len * along[i] for i in range(2))
            applied = apply_op(residual)
            norm_next, product = total(residual, residual), total(residual, applied)
            beta_ratio = norm_next / norm_now
            step_len = norm_next / (product - beta_ratio * norm_next / step_len)
            own_direction = own_residual + beta_ratio * own_direction
            own_along = own(applied) + beta_ratio * own_along
            if sweep + 2 < ITERS:
                along = tuple(applied[i] + beta_ratio * along[i] for i in range(2))
            norm_now = norm_next
    surface_ref[...] = own_surface
    residual_ref[...] = own_residual


VMEM_SPEC = pl.BlockSpec(memory_space=pltpu.VMEM)
SMEM_SPEC = pl.BlockSpec(memory_space=pltpu.SMEM)
SMALL_GRANT = pltpu.CompilerParams(vmem_limit_bytes=8 << 20)


def tile_shape(rows):
    return jax.ShapeDtypeStruct((rows, LANE), jnp.float32)


def small_shards(tracers, velocity, depth_levels, vdiff):
    count = tracers.shape[1]
    blocks = lax.axis_size("blk")
    devices = blocks * 2
    rows = 2 * count * SUB
    halo_rows = 3 * count + SUB

    sums, near, far, tracer_rows, velocity_rows, depth = pl.pallas_call(
        functools.partial(pack_kernel, count),
        out_shape=[
            tile_shape(3 * SUB),
            tile_shape(halo_rows + 2 * SUB),
            tile_shape(halo_rows),
            tile_shape(rows),
            tile_shape(rows),
            jax.ShapeDtypeStruct((SUB, LANE), jnp.int32),
        ],
        in_specs=[pl.BlockSpec(memory_space=pltpu.HBM)] * 3,
        out_specs=[VMEM_SPEC] * 6,
        scratch_shapes=[pltpu.SemaphoreType.DMA((3,))],
        compiler_params=SMALL_GRANT,
        name="pack",
    )(*(pltpu.with_memory_space_constraint(x, pltpu.HBM) for x in (tracers.reshape(rows, LANE), velocity.reshape(rows, LANE), depth_levels)))

    near = lax.ppermute(near, AXES, [(i, i ^ 2) for i in range(devices)])
    far_pairs = []
    for blk in range(1, blocks, 2):
        for grp in range(2):
            here = blk * 2 + grp
            far_pairs += [(here, here ^ 1)] if blk == blocks - 1 else [(here, here + 2), (here + 2, here)]
    far = lax.ppermute(far, AXES, far_pairs + [(0, 1), (1, 0)])

    order = [*range(devices.bit_length() - 2, 2, -1), 0, 2]
    gathered, edges = sums, None
    for bit in order:
        pairs = [(i, i ^ (1 << bit | 2)) for i in range(devices)]
        if bit == 0:
            edges = lax.ppermute(jnp.concatenate([gathered, near[halo_rows:]], 0), AXES, pairs)
            came = edges[: gathered.shape[0]]
        else:
            came = lax.ppermute(gathered, AXES, pairs)
        gathered = jnp.concatenate([gathered, came], 0)
    other = lax.ppermute(gathered, AXES, [(i, i ^ 2) for i in range(devices)])

    new_rows = pl.pallas_call(
        functools.partial(tracer_kernel, count, blocks),
        out_shape=tile_shape(rows),
        in_specs=[SMEM_SPEC] + [VMEM_SPEC] * 6,
        out_specs=VMEM_SPEC,
        compiler_params=SMALL_GRANT,
        name="tracer",
    )(vdiff, tracer_rows, velocity_rows, depth, near, far, edges)

    slots = devices // 2
    surface, residual = pl.pallas_call(
        functools.partial(solve_kernel, count, blocks, tuple(order)),
        out_shape=[tile_shape(SUB), tile_shape(SUB)],
        in_specs=[VMEM_SPEC] * 2,
        out_specs=[VMEM_SPEC] * 2,
        scratch_shapes=[pltpu.VMEM((2, blocks * SUB, LANE), jnp.float32)],
        compiler_params=SMALL_GRANT,
        name="solve",
    )(gathered.reshape(slots, 3 * SUB, LANE), other.reshape(slots, 3 * SUB, LANE))
    return new_rows.reshape(tracers.shape), surface, residual


def shards(tracers, velocity, depth_levels, vdiff):
    blocks, groups = lax.axis_size("blk"), lax.axis_size("grp")
    height, breadth = depth_levels.shape
    tiled = (height, breadth) == (SUB, LANE) and groups == 2 and blocks >= 4 and blocks & (blocks - 1) == 0
    if tiled and 3 * tracers.shape[1] < LANE and blocks * groups * SUB * LANE <= GATHER_CELLS:
        return small_shards(tracers, velocity, depth_levels, vdiff)
    return wide_shards(tracers, velocity, depth_levels, vdiff)


def solution(mesh):
    return jax.shard_map(
        shards,
        mesh=mesh,
        in_specs=(P(None, None, "blk", "grp"), P(None, None, "blk", "grp"), P("blk", "grp"), P()),
        out_specs=(P(None, None, "blk", "grp"), P("blk", "grp"), P("blk", "grp")),
        check_vma=False,
    )
```

```python
import functools

import jax
import jax.numpy as jnp
from jax import lax
from jax.experimental import pallas as pl
from jax.experimental.pallas import tpu as pltpu
from jax.sharding import PartitionSpec as P


ITERS = 3


TIME_STEP = 0.2
MIX_COEF = 0.25
SEA_DIAG = 0.5

AXES = ("blk", "grp")
GATHER_CELLS = 1 << 17


def swapped(value, axis, stride):
    return lax.ppermute(value, axis, [(i, i ^ 1 << stride) for i in range(lax.axis_size(axis))])


def padded_2(cells, sides, width, closed):
    for axis, dim in sides:
        count = lax.axis_size(axis)
        ends = count if closed else count - 1
        head = lax.slice_in_dim(cells, 0, width, axis=dim)
        tail = lax.slice_in_dim(cells, cells.shape[dim] - width, cells.shape[dim], axis=dim)
        cells = jnp.concatenate(
            [
                lax.ppermute(tail, axis, [(i, (i + 1) % count) for i in range(ends)]),
                cells,
                lax.ppermute(head, axis, [((i + 1) % count, i) for i in range(ends)]),
            ],
            axis=dim,
        )
    return cells


def tracer_step(tracer, velocity, depth_pad, vdiff):
    count = tracer.shape[1]
    levels = jnp.arange(count, dtype=jnp.float32)[:, None, None]
    wet_mask = (levels < depth_pad[None]).astype(jnp.float32)
    east_vel = velocity[0]
    north_vel = velocity[1]
    row_set = tracer[:, :, 1:-1, :]
    wet_rows = wet_mask[:, 1:-1, :]
    east_rows = east_vel[:, 1:-1, :]
    east_open = wet_rows[:, :, :-1] * wet_rows[:, :, 1:]
    east_face = 0.5 * (east_rows[:, :, :-1] + east_rows[:, :, 1:])
    east_flux = east_open * (
        east_face * 0.5 * (row_set[..., :-1] + row_set[..., 1:])
        - MIX_COEF * (row_set[..., 1:] - row_set[..., :-1])
    )
    col_set = tracer[:, :, :, 1:-1]
    wet_cols = wet_mask[:, :, 1:-1]
    north_cols = north_vel[:, :, 1:-1]
    north_open = wet_cols[:, :-1, :] * wet_cols[:, 1:, :]
    north_face = 0.5 * (north_cols[:, :-1, :] + north_cols[:, 1:, :])
    north_flux = north_open * (
        north_face * 0.5 * (col_set[:, :, :-1, :] + col_set[:, :, 1:, :])
        - MIX_COEF * (col_set[:, :, 1:, :] - col_set[:, :, :-1, :])
    )
    centre = tracer[:, :, 1:-1, 1:-1]
    wet_centre = wet_mask[:, 1:-1, 1:-1]
    vert_open = wet_centre[:-1] * wet_centre[1:]
    vert_flux = vdiff[:, None, None] * vert_open * (centre[:, 1:] - centre[:, :-1])
    border = jnp.zeros_like(centre[:, :1])
    vert_flux = jnp.concatenate([border, vert_flux, border], 1)
    tendency = (
        vert_flux[:, 1:]
        - vert_flux[:, :-1]
        - (east_flux[..., 1:] - east_flux[..., :-1])
        - (north_flux[:, :, 1:, :] - north_flux[:, :, :-1, :])
    )
    return wet_centre * (centre + TIME_STEP * tendency)


def column_forcing(velocity, depth_pad):
    count = velocity.shape[1]
    levels = jnp.arange(count, dtype=jnp.float32)[:, None, None]
    wet_mask = (levels < depth_pad[None]).astype(jnp.float32)
    east_sum = jnp.sum(wet_mask * velocity[0], 0)
    north_sum = jnp.sum(wet_mask * velocity[1], 0)
    ocean_mask = (depth_pad[1:-1, 1:-1] > 0).astype(jnp.float32)
    return ocean_mask * (
        0.5 * (east_sum[1:-1, 2:] - east_sum[1:-1, :-2])
        + 0.5 * (north_sum[2:, 1:-1] - north_sum[:-2, 1:-1])
    )


def sea_operator(field_pad, depth_pad, count):
    centre = field_pad[1:-1, 1:-1]
    depth_c = depth_pad[1:-1, 1:-1]
    ocean_mask = (depth_c > 0).astype(jnp.float32)
    total = SEA_DIAG * centre
    for rows_at, cols_at in (
        (slice(1, -1), slice(2, None)),
        (slice(1, -1), slice(None, -2)),
        (slice(2, None), slice(1, -1)),
        (slice(None, -2), slice(1, -1)),
    ):
        weight = jnp.minimum(depth_c, depth_pad[rows_at, cols_at]) / count
        total = total + weight * (centre - field_pad[rows_at, cols_at])
    return ocean_mask * total + (1.0 - ocean_mask) * centre


def extend(fields, fold_sign):
    top_row = fields[:, -1, :]
    partner = top_row
    for bit_index in range(lax.axis_size("grp").bit_length() - 1):
        partner = swapped(partner, "grp", bit_index)
    mirror = partner[:, ::-1]
    northmost = lax.axis_index("blk") == lax.axis_size("blk") - 1
    row_halo = padded_2(fields, (("blk", 1),), 1, False)
    north_row = jnp.where(northmost, mirror * fold_sign[:, None], row_halo[:, -1, :])
    grown = jnp.concatenate([row_halo[:, :-1, :], north_row[:, None, :]], 1)
    return padded_2(grown, (("grp", 2),), 1, True)


def two_sums(residual, applied):
    return lax.psum((jnp.sum(residual * residual), jnp.sum(residual * applied)), AXES)


def wide_shards(tracers, velocity, depth_levels, vdiff):
    count = tracers.shape[1]
    height, breadth = depth_levels.shape
    fields = jnp.concatenate(
        [
            tracers.reshape(2 * count, height, breadth),
            velocity.reshape(2 * count, height, breadth),
            depth_levels.astype(jnp.float32)[None],
        ],
        0,
    )
    fold_sign = jnp.concatenate(
        [
            jnp.ones((2 * count,), jnp.float32),
            -jnp.ones((2 * count,), jnp.float32),
            jnp.ones((1,), jnp.float32),
        ]
    )
    padded = extend(fields, fold_sign)
    tracer_pad = padded[: 2 * count].reshape(2, count, height + 2, breadth + 2)
    velocity_pad = padded[2 * count : 4 * count].reshape(2, count, height + 2, breadth + 2)
    depth_pad = padded[4 * count]
    new_tracers = tracer_step(tracer_pad, velocity_pad, depth_pad, vdiff)
    forcing = column_forcing(velocity_pad, depth_pad)

    def apply_op(field):
        grown = extend(field[None], jnp.ones((1,), jnp.float32))[0]
        return sea_operator(grown, depth_pad, count)

    surface = jnp.zeros_like(forcing)
    residual = forcing
    applied = apply_op(residual)
    norm_now, product = two_sums(residual, applied)
    step_len = norm_now / product
    direction, along = (residual, applied)
    for sweep in range(ITERS):
        surface = surface + step_len * direction
        residual = residual - step_len * along
        if sweep + 1 < ITERS:
            applied = apply_op(residual)
            norm_next, product = two_sums(residual, applied)
            beta_ratio = norm_next / norm_now
            step_len = norm_next / (product - beta_ratio * norm_next / step_len)
            direction = residual + beta_ratio * direction
            along = applied + beta_ratio * along
            norm_now = norm_next
    return (new_tracers, surface, residual)


SUB, LANE = 8, 128


def tile_iota(dim):
    return lax.broadcasted_iota(jnp.int32, (SUB, LANE), dim)


def reversed_lanes(value):
    index = LANE - 1 - lax.broadcasted_iota(jnp.int32, value.shape, 1)
    return jnp.take_along_axis(value, index, axis=1)


def sums_kernel(count, tracers_hbm, velocity_hbm, depth_hbm, sums_ref, tracers_ref, velocity_ref, depth_ref, sems):
    copies = [
        pltpu.make_async_copy(src, dst, sems.at[at])
        for at, (src, dst) in enumerate(
            ((depth_hbm, depth_ref), (velocity_hbm, velocity_ref), (tracers_hbm, tracers_ref))
        )
    ]
    for copy in copies:
        copy.start()
    copies[0].wait()
    copies[1].wait()
    depth = depth_ref[...]
    east = jnp.zeros((SUB, LANE), jnp.float32)
    north = jnp.zeros((SUB, LANE), jnp.float32)
    for level in range(count):
        wet = depth > level
        east += jnp.where(wet, velocity_ref[pl.ds(level * SUB, SUB), :], 0.0)
        north += jnp.where(wet, velocity_ref[pl.ds((count + level) * SUB, SUB), :], 0.0)
    sums_ref[0:SUB, :] = east
    sums_ref[SUB : 2 * SUB, :] = north
    sums_ref[2 * SUB : 3 * SUB, :] = depth.astype(jnp.float32)
    copies[2].wait()


def pack_kernel(count, tracers_ref, velocity_ref, depth_ref, near_ref, far_ref):
    odd = lax.axis_index("blk") % 2 == 1
    depth = depth_ref[...].astype(jnp.float32)

    def both(ref, first, rows):
        low = ref[pl.ds(first, rows, stride=SUB), :]
        high = ref[pl.ds(first + SUB - 1, rows, stride=SUB), :]
        return jnp.where(odd, low, high), jnp.where(odd, high, low)

    depth_low = jnp.broadcast_to(depth[0:1, :], (SUB, LANE))
    depth_high = jnp.broadcast_to(depth[SUB - 1 : SUB, :], (SUB, LANE))
    parts = (
        both(tracers_ref, 0, 2 * count),
        both(velocity_ref, count * SUB, count),
        (jnp.where(odd, depth_low, depth_high), jnp.where(odd, depth_high, depth_low)),
    )
    at = 0
    for near, far in parts:
        near_ref[at : at + near.shape[0], :] = near
        far_ref[at : at + near.shape[0], :] = far
        at += near.shape[0]
    lane = tile_iota(1)
    west_pack = jnp.zeros((SUB, LANE), jnp.float32)
    east_pack = jnp.zeros((SUB, LANE), jnp.float32)
    for field in range(3 * count + 1):
        if field < 2 * count:
            tile = tracers_ref[pl.ds(field * SUB, SUB), :]
        elif field < 3 * count:
            tile = velocity_ref[pl.ds((field - 2 * count) * SUB, SUB), :]
        else:
            tile = depth
        west_pack = jnp.where(lane == field, pltpu.roll(tile, field, 1), west_pack)
        east_pack = jnp.where(lane == field, pltpu.roll(tile, field + 1, 1), east_pack)
    near_ref[at : at + SUB, :] = west_pack
    near_ref[at + SUB : at + 2 * SUB, :] = east_pack


def tracer_kernel(
    count, blocks, vdiff_ref, tracers_ref, velocity_ref, depth_ref, near_ref, far_ref, edge_ref, out_ref
):
    blk = lax.axis_index("blk")
    odd = blk % 2 == 1
    fold = blk == blocks - 1
    lane, sub = tile_iota(1), tile_iota(0)
    rows = far_ref.shape[0]
    near = near_ref[0:rows, :]
    far = jnp.where(blk == 0, 0.0, far_ref[...])
    row_id = lax.broadcasted_iota(jnp.int32, (rows, LANE), 0)
    sign = jnp.where((row_id >= 2 * count) & (row_id < 3 * count), -1.0, 1.0)
    far_north = jnp.where(fold, reversed_lanes(far) * sign, far)
    north_rows = jnp.where(odd, far_north, near)
    south_rows = jnp.where(odd, near, far)
    edge_base = edge_ref.shape[0] - 2 * SUB
    east_cols = edge_ref[edge_base : edge_base + SUB, :]
    west_cols = edge_ref[edge_base + SUB : edge_base + 2 * SUB, :]

    def spread(packed, field, at):
        return pltpu.roll(packed, (at - field) % LANE, 1)

    def east_of(tile, field):
        return jnp.where(lane == LANE - 1, spread(east_cols, field, LANE - 1), pltpu.roll(tile, LANE - 1, 1))

    def west_of(tile, field):
        return jnp.where(lane == 0, spread(west_cols, field, 0), pltpu.roll(tile, 1, 1))

    def north_of(tile, field):
        ghost = jnp.broadcast_to(north_rows[field : field + 1, :], (SUB, LANE))
        return jnp.where(sub == SUB - 1, ghost, pltpu.roll(tile, SUB - 1, 0))

    def south_of(tile, field):
        ghost = jnp.broadcast_to(south_rows[field : field + 1, :], (SUB, LANE))
        return jnp.where(sub == 0, ghost, pltpu.roll(tile, 1, 0))

    depth = depth_ref[...].astype(jnp.float32)
    at = 3 * count
    open_east = jnp.minimum(depth, east_of(depth, at))
    open_west = jnp.minimum(depth, west_of(depth, at))
    open_north = jnp.minimum(depth, north_of(depth, at))
    open_south = jnp.minimum(depth, south_of(depth, at))

    def flux(here, there, speed):
        return speed * (there + here) - MIX_COEF * (there - here)

    below = [None, None]
    for level in range(count):
        u = velocity_ref[pl.ds(level * SUB, SUB), :]
        v = velocity_ref[pl.ds((count + level) * SUB, SUB), :]
        k = float(level)
        east_speed = 0.25 * (u + east_of(u, 2 * count + level))
        west_speed = 0.25 * (u + west_of(u, 2 * count + level))
        north_speed = 0.25 * (v + north_of(v, 2 * count + level))
        south_speed = 0.25 * (v + south_of(v, 2 * count + level))
        for which in range(2):
            field = which * count + level
            here = tracers_ref[pl.ds(field * SUB, SUB), :]
            out = jnp.where(open_east > k, flux(here, east_of(here, field), east_speed), 0.0)
            out -= jnp.where(open_west > k, flux(west_of(here, field), here, west_speed), 0.0)
            out += jnp.where(open_north > k, flux(here, north_of(here, field), north_speed), 0.0)
            out -= jnp.where(open_south > k, flux(south_of(here, field), here, south_speed), 0.0)
            tendency = -out
            if level + 1 < count:
                under = tracers_ref[pl.ds((field + 1) * SUB, SUB), :]
                vertical = jnp.where(depth > k + 1.0, vdiff_ref[level] * (under - here), 0.0)
                tendency += vertical
            else:
                vertical = None
            if below[which] is not None:
                tendency -= below[which]
            below[which] = vertical
            out_ref[pl.ds(field * SUB, SUB), :] = jnp.where(depth > k, here + TIME_STEP * tendency, 0.0)


def solve_kernel(
    count, blocks, apart, own_ref, other_ref, rows_ref, surface_ref, residual_ref, rows_hbm, fields, scratch, sem
):
    leaving = pltpu.make_async_copy(rows_ref, rows_hbm, sem)
    leaving.start()
    me = lax.axis_index("blk") * 2 + lax.axis_index("grp")
    height = blocks * SUB

    for slot, mask in enumerate(apart):
        fields[me ^ mask] = own_ref[slot]
        fields[me ^ (mask ^ 2)] = other_ref[slot]

    def field(part):
        rows = slice(part * SUB, (part + 1) * SUB)
        return tuple(
            jnp.concatenate([fields[blk * 2 + grp, rows, :] for blk in range(blocks)], 0) for grp in range(2)
        )

    shape = (height, LANE)
    lane = lax.broadcasted_iota(jnp.int32, shape, 1)
    sub = tile_iota(0)

    def east_of(pair):
        low, high = (pltpu.roll(half, LANE - 1, 1) for half in pair)
        return jnp.where(lane == LANE - 1, high, low), jnp.where(lane == LANE - 1, low, high)

    def west_of(pair):
        low, high = (pltpu.roll(half, 1, 1) for half in pair)
        return jnp.where(lane == 0, high, low), jnp.where(lane == 0, low, high)

    def north_of(pair, sign=1.0):
        out = []
        for half, mirror in zip(pair, pair[::-1]):
            moved = pltpu.roll(half, height - 1, 0)
            ghost = reversed_lanes(mirror[height - SUB :, :]) * sign
            top = jnp.where(sub == SUB - 1, ghost, moved[height - SUB :, :])
            out.append(jnp.concatenate([moved[: height - SUB, :], top], 0))
        return tuple(out)

    def south_of(pair):
        out = []
        for half in pair:
            moved = pltpu.roll(half, 1, 0)
            bottom = jnp.where(sub == 0, 0.0, moved[:SUB, :])
            out.append(jnp.concatenate([bottom, moved[SUB:, :]], 0))
        return tuple(out)

    u, v, depth = field(0), field(1), field(2)
    weight_east = tuple(jnp.minimum(a, b) * (1.0 / count) for a, b in zip(depth, east_of(depth)))
    weight_north = tuple(jnp.minimum(a, b) * (1.0 / count) for a, b in zip(depth, north_of(depth)))
    diagonal = tuple(jnp.where(d > 0.0, SEA_DIAG, 1.0) for d in depth)

    ue, uw, vn, vs = east_of(u), west_of(u), north_of(v, -1.0), south_of(v)
    forcing = tuple(
        jnp.where(depth[i] > 0.0, 0.5 * (ue[i] - uw[i]) + 0.5 * (vn[i] - vs[i]), 0.0) for i in range(2)
    )

    def apply_op(x):
        xe, xn = east_of(x), north_of(x)
        flux_e = tuple(weight_east[i] * (xe[i] - x[i]) for i in range(2))
        flux_n = tuple(weight_north[i] * (xn[i] - x[i]) for i in range(2))
        fw, fs = west_of(flux_e), south_of(flux_n)
        return tuple(diagonal[i] * x[i] - (flux_e[i] - fw[i]) - (flux_n[i] - fs[i]) for i in range(2))

    def total(a, b):
        part = a[0] * b[0] + a[1] * b[1]
        return jnp.sum(jnp.sum(part.reshape(blocks, SUB, LANE), 0), keepdims=True)

    grp = me % 2
    mine = pl.ds(pl.multiple_of((me // 2) * SUB, SUB), SUB)

    def own(pair):
        scratch[0] = pair[0]
        scratch[1] = pair[1]
        return jnp.where(grp == 0, scratch[0, mine, :], scratch[1, mine, :])

    residual = forcing
    applied = apply_op(residual)
    norm_now, product = total(residual, residual), total(residual, applied)
    step_len = norm_now / product
    along = applied
    own_residual = own(residual)
    own_along = own(applied)
    own_direction = own_residual
    own_surface = jnp.zeros((SUB, LANE), jnp.float32)
    for sweep in range(ITERS):
        own_surface = own_surface + step_len * own_direction
        own_residual = own_residual - step_len * own_along
        if sweep + 1 < ITERS:
            residual = tuple(residual[i] - step_len * along[i] for i in range(2))
            applied = apply_op(residual)
            norm_next, product = total(residual, residual), total(residual, applied)
            beta_ratio = norm_next / norm_now
            step_len = norm_next / (product - beta_ratio * norm_next / step_len)
            own_direction = own_residual + beta_ratio * own_direction
            own_along = own(applied) + beta_ratio * own_along
            if sweep + 2 < ITERS:
                along = tuple(applied[i] + beta_ratio * along[i] for i in range(2))
            norm_now = norm_next
    surface_ref[...] = own_surface
    residual_ref[...] = own_residual
    leaving.wait()


VMEM_SPEC = pl.BlockSpec(memory_space=pltpu.VMEM)
SMEM_SPEC = pl.BlockSpec(memory_space=pltpu.SMEM)
SMALL_GRANT = pltpu.CompilerParams(vmem_limit_bytes=8 << 20)


def tile_shape(rows):
    return jax.ShapeDtypeStruct((rows, LANE), jnp.float32)


def gather_stages(devices):
    single = [(1 << bit | 2,) for bit in range(devices.bit_length() - 2, 2, -1)]
    return [*single, (7, 3, 6)]


def small_shards(tracers, velocity, depth_levels, vdiff):
    count = tracers.shape[1]
    blocks = lax.axis_size("blk")
    devices = blocks * 2
    rows = 2 * count * SUB
    halo_rows = 3 * count + SUB

    arguments = (tracers.reshape(rows, LANE), velocity.reshape(rows, LANE), depth_levels)
    sums, tracer_rows, velocity_rows, depth = pl.pallas_call(
        functools.partial(sums_kernel, count),
        out_shape=[
            tile_shape(3 * SUB),
            tile_shape(rows),
            tile_shape(rows),
            jax.ShapeDtypeStruct((SUB, LANE), jnp.int32),
        ],
        in_specs=[pl.BlockSpec(memory_space=pltpu.HBM)] * 3,
        out_specs=[VMEM_SPEC] * 4,
        scratch_shapes=[pltpu.SemaphoreType.DMA((3,))],
        compiler_params=SMALL_GRANT,
        name="sums",
    )(*(pltpu.with_memory_space_constraint(x, pltpu.HBM) for x in arguments))
    near, far = pl.pallas_call(
        functools.partial(pack_kernel, count),
        out_shape=[tile_shape(halo_rows + 2 * SUB), tile_shape(halo_rows)],
        in_specs=[VMEM_SPEC] * 3,
        out_specs=[VMEM_SPEC] * 2,
        compiler_params=SMALL_GRANT,
        name="pack",
    )(tracer_rows, velocity_rows, depth)

    near = lax.ppermute(near, AXES, [(i, i ^ 2) for i in range(devices)])
    far_pairs = []
    for blk in range(1, blocks, 2):
        for grp in range(2):
            here = blk * 2 + grp
            far_pairs += [(here, here ^ 1)] if blk == blocks - 1 else [(here, here + 2), (here + 2, here)]
    far = lax.ppermute(far, AXES, far_pairs + [(0, 1), (1, 0)])

    gathered, edges, apart = sums, None, [0]
    for masks in gather_stages(devices):
        pieces = [gathered]
        for mask in masks:
            pairs = [(i, i ^ mask) for i in range(devices)]
            if mask & 1:
                edges = lax.ppermute(jnp.concatenate([gathered, near[halo_rows:]], 0), AXES, pairs)
                pieces.append(edges[: gathered.shape[0]])
            else:
                pieces.append(lax.ppermute(gathered, AXES, pairs))
        gathered = jnp.concatenate(pieces, 0)
        apart = apart + [came ^ mask for mask in masks for came in apart]
    other = lax.ppermute(gathered, AXES, [(i, i ^ 2) for i in range(devices)])

    new_rows = pl.pallas_call(
        functools.partial(tracer_kernel, count, blocks),
        out_shape=pltpu.VMEM((rows, LANE), jnp.float32),
        in_specs=[SMEM_SPEC] + [VMEM_SPEC] * 6,
        out_specs=VMEM_SPEC,
        compiler_params=SMALL_GRANT,
        name="tracer",
    )(vdiff, tracer_rows, velocity_rows, depth, near, far, edges)

    slots = devices // 2
    surface, residual, new_rows = pl.pallas_call(
        functools.partial(solve_kernel, count, blocks, tuple(apart)),
        out_shape=[tile_shape(SUB), tile_shape(SUB), tile_shape(rows)],
        in_specs=[VMEM_SPEC] * 3,
        out_specs=[VMEM_SPEC, VMEM_SPEC, pl.BlockSpec(memory_space=pltpu.HBM)],
        scratch_shapes=[
            pltpu.VMEM((devices, 3 * SUB, LANE), jnp.float32),
            pltpu.VMEM((2, blocks * SUB, LANE), jnp.float32),
            pltpu.SemaphoreType.DMA,
        ],
        compiler_params=SMALL_GRANT,
        name="solve",
    )(gathered.reshape(slots, 3 * SUB, LANE), other.reshape(slots, 3 * SUB, LANE), new_rows)
    return new_rows.reshape(tracers.shape), surface, residual


def shards(tracers, velocity, depth_levels, vdiff):
    blocks, groups = lax.axis_size("blk"), lax.axis_size("grp")
    height, breadth = depth_levels.shape
    tiled = (height, breadth) == (SUB, LANE) and groups == 2 and blocks >= 4 and blocks & (blocks - 1) == 0
    if tiled and 3 * tracers.shape[1] < LANE and blocks * groups * SUB * LANE <= GATHER_CELLS:
        return small_shards(tracers, velocity, depth_levels, vdiff)
    return wide_shards(tracers, velocity, depth_levels, vdiff)


def solution(mesh):
    return jax.shard_map(
        shards,
        mesh=mesh,
        in_specs=(P(None, None, "blk", "grp"), P(None, None, "blk", "grp"), P("blk", "grp"), P()),
        out_specs=(P(None, None, "blk", "grp"), P("blk", "grp"), P("blk", "grp")),
        check_vma=False,
    )
```

```python
import functools

import jax
import jax.numpy as jnp
from jax import lax
from jax.experimental import pallas as pl
from jax.experimental.pallas import tpu as pltpu
from jax.sharding import PartitionSpec as P


ITERS = 3


TIME_STEP = 0.2
MIX_COEF = 0.25
SEA_DIAG = 0.5

AXES = ("blk", "grp")
GATHER_CELLS = 1 << 17


def swapped(value, axis, stride):
    return lax.ppermute(value, axis, [(i, i ^ 1 << stride) for i in range(lax.axis_size(axis))])


def padded_2(cells, sides, width, closed):
    for axis, dim in sides:
        count = lax.axis_size(axis)
        ends = count if closed else count - 1
        head = lax.slice_in_dim(cells, 0, width, axis=dim)
        tail = lax.slice_in_dim(cells, cells.shape[dim] - width, cells.shape[dim], axis=dim)
        cells = jnp.concatenate(
            [
                lax.ppermute(tail, axis, [(i, (i + 1) % count) for i in range(ends)]),
                cells,
                lax.ppermute(head, axis, [((i + 1) % count, i) for i in range(ends)]),
            ],
            axis=dim,
        )
    return cells


def tracer_step(tracer, velocity, depth_pad, vdiff):
    count = tracer.shape[1]
    levels = jnp.arange(count, dtype=jnp.float32)[:, None, None]
    wet_mask = (levels < depth_pad[None]).astype(jnp.float32)
    east_vel = velocity[0]
    north_vel = velocity[1]
    row_set = tracer[:, :, 1:-1, :]
    wet_rows = wet_mask[:, 1:-1, :]
    east_rows = east_vel[:, 1:-1, :]
    east_open = wet_rows[:, :, :-1] * wet_rows[:, :, 1:]
    east_face = 0.5 * (east_rows[:, :, :-1] + east_rows[:, :, 1:])
    east_flux = east_open * (
        east_face * 0.5 * (row_set[..., :-1] + row_set[..., 1:])
        - MIX_COEF * (row_set[..., 1:] - row_set[..., :-1])
    )
    col_set = tracer[:, :, :, 1:-1]
    wet_cols = wet_mask[:, :, 1:-1]
    north_cols = north_vel[:, :, 1:-1]
    north_open = wet_cols[:, :-1, :] * wet_cols[:, 1:, :]
    north_face = 0.5 * (north_cols[:, :-1, :] + north_cols[:, 1:, :])
    north_flux = north_open * (
        north_face * 0.5 * (col_set[:, :, :-1, :] + col_set[:, :, 1:, :])
        - MIX_COEF * (col_set[:, :, 1:, :] - col_set[:, :, :-1, :])
    )
    centre = tracer[:, :, 1:-1, 1:-1]
    wet_centre = wet_mask[:, 1:-1, 1:-1]
    vert_open = wet_centre[:-1] * wet_centre[1:]
    vert_flux = vdiff[:, None, None] * vert_open * (centre[:, 1:] - centre[:, :-1])
    border = jnp.zeros_like(centre[:, :1])
    vert_flux = jnp.concatenate([border, vert_flux, border], 1)
    tendency = (
        vert_flux[:, 1:]
        - vert_flux[:, :-1]
        - (east_flux[..., 1:] - east_flux[..., :-1])
        - (north_flux[:, :, 1:, :] - north_flux[:, :, :-1, :])
    )
    return wet_centre * (centre + TIME_STEP * tendency)


def column_forcing(velocity, depth_pad):
    count = velocity.shape[1]
    levels = jnp.arange(count, dtype=jnp.float32)[:, None, None]
    wet_mask = (levels < depth_pad[None]).astype(jnp.float32)
    east_sum = jnp.sum(wet_mask * velocity[0], 0)
    north_sum = jnp.sum(wet_mask * velocity[1], 0)
    ocean_mask = (depth_pad[1:-1, 1:-1] > 0).astype(jnp.float32)
    return ocean_mask * (
        0.5 * (east_sum[1:-1, 2:] - east_sum[1:-1, :-2])
        + 0.5 * (north_sum[2:, 1:-1] - north_sum[:-2, 1:-1])
    )


def sea_operator(field_pad, depth_pad, count):
    centre = field_pad[1:-1, 1:-1]
    depth_c = depth_pad[1:-1, 1:-1]
    ocean_mask = (depth_c > 0).astype(jnp.float32)
    total = SEA_DIAG * centre
    for rows_at, cols_at in (
        (slice(1, -1), slice(2, None)),
        (slice(1, -1), slice(None, -2)),
        (slice(2, None), slice(1, -1)),
        (slice(None, -2), slice(1, -1)),
    ):
        weight = jnp.minimum(depth_c, depth_pad[rows_at, cols_at]) / count
        total = total + weight * (centre - field_pad[rows_at, cols_at])
    return ocean_mask * total + (1.0 - ocean_mask) * centre


def extend(fields, fold_sign):
    top_row = fields[:, -1, :]
    partner = top_row
    for bit_index in range(lax.axis_size("grp").bit_length() - 1):
        partner = swapped(partner, "grp", bit_index)
    mirror = partner[:, ::-1]
    northmost = lax.axis_index("blk") == lax.axis_size("blk") - 1
    row_halo = padded_2(fields, (("blk", 1),), 1, False)
    north_row = jnp.where(northmost, mirror * fold_sign[:, None], row_halo[:, -1, :])
    grown = jnp.concatenate([row_halo[:, :-1, :], north_row[:, None, :]], 1)
    return padded_2(grown, (("grp", 2),), 1, True)


def two_sums(residual, applied):
    return lax.psum((jnp.sum(residual * residual), jnp.sum(residual * applied)), AXES)


def wide_shards(tracers, velocity, depth_levels, vdiff):
    count = tracers.shape[1]
    height, breadth = depth_levels.shape
    fields = jnp.concatenate(
        [
            tracers.reshape(2 * count, height, breadth),
            velocity.reshape(2 * count, height, breadth),
            depth_levels.astype(jnp.float32)[None],
        ],
        0,
    )
    fold_sign = jnp.concatenate(
        [
            jnp.ones((2 * count,), jnp.float32),
            -jnp.ones((2 * count,), jnp.float32),
            jnp.ones((1,), jnp.float32),
        ]
    )
    padded = extend(fields, fold_sign)
    tracer_pad = padded[: 2 * count].reshape(2, count, height + 2, breadth + 2)
    velocity_pad = padded[2 * count : 4 * count].reshape(2, count, height + 2, breadth + 2)
    depth_pad = padded[4 * count]
    new_tracers = tracer_step(tracer_pad, velocity_pad, depth_pad, vdiff)
    forcing = column_forcing(velocity_pad, depth_pad)

    def apply_op(field):
        grown = extend(field[None], jnp.ones((1,), jnp.float32))[0]
        return sea_operator(grown, depth_pad, count)

    surface = jnp.zeros_like(forcing)
    residual = forcing
    applied = apply_op(residual)
    norm_now, product = two_sums(residual, applied)
    step_len = norm_now / product
    direction, along = (residual, applied)
    for sweep in range(ITERS):
        surface = surface + step_len * direction
        residual = residual - step_len * along
        if sweep + 1 < ITERS:
            applied = apply_op(residual)
            norm_next, product = two_sums(residual, applied)
            beta_ratio = norm_next / norm_now
            step_len = norm_next / (product - beta_ratio * norm_next / step_len)
            direction = residual + beta_ratio * direction
            along = applied + beta_ratio * along
            norm_now = norm_next
    return (new_tracers, surface, residual)


SUB, LANE = 8, 128


def tile_iota(dim):
    return lax.broadcasted_iota(jnp.int32, (SUB, LANE), dim)


def reversed_lanes(value):
    index = LANE - 1 - lax.broadcasted_iota(jnp.int32, value.shape, 1)
    return jnp.take_along_axis(value, index, axis=1)


def sums_kernel(count, tracers_hbm, velocity_hbm, depth_hbm, sums_ref, tracers_ref, velocity_ref, depth_ref, sems):
    copies = [
        pltpu.make_async_copy(src, dst, sems.at[at])
        for at, (src, dst) in enumerate(
            ((depth_hbm, depth_ref), (velocity_hbm, velocity_ref), (tracers_hbm, tracers_ref))
        )
    ]
    for copy in copies:
        copy.start()
    copies[0].wait()
    copies[1].wait()
    depth = depth_ref[...]
    east = jnp.zeros((SUB, LANE), jnp.float32)
    north = jnp.zeros((SUB, LANE), jnp.float32)
    for level in range(count):
        wet = depth > level
        east += jnp.where(wet, velocity_ref[pl.ds(level * SUB, SUB), :], 0.0)
        north += jnp.where(wet, velocity_ref[pl.ds((count + level) * SUB, SUB), :], 0.0)
    sums_ref[0:SUB, :] = east
    sums_ref[SUB : 2 * SUB, :] = north
    sums_ref[2 * SUB : 3 * SUB, :] = depth.astype(jnp.float32)
    copies[2].wait()


def pack_kernel(count, tracers_ref, velocity_ref, depth_ref, near_ref, far_ref):
    odd = lax.axis_index("blk") % 2 == 1
    depth = depth_ref[...].astype(jnp.float32)

    def both(ref, first, rows):
        low = ref[pl.ds(first, rows, stride=SUB), :]
        high = ref[pl.ds(first + SUB - 1, rows, stride=SUB), :]
        return jnp.where(odd, low, high), jnp.where(odd, high, low)

    depth_low = jnp.broadcast_to(depth[0:1, :], (SUB, LANE))
    depth_high = jnp.broadcast_to(depth[SUB - 1 : SUB, :], (SUB, LANE))
    parts = (
        both(tracers_ref, 0, 2 * count),
        both(velocity_ref, count * SUB, count),
        (jnp.where(odd, depth_low, depth_high), jnp.where(odd, depth_high, depth_low)),
    )
    at = 0
    for near, far in parts:
        near_ref[at : at + near.shape[0], :] = near
        far_ref[at : at + near.shape[0], :] = far
        at += near.shape[0]
    lane = tile_iota(1)
    west_pack = jnp.zeros((SUB, LANE), jnp.float32)
    east_pack = jnp.zeros((SUB, LANE), jnp.float32)
    for field in range(3 * count + 1):
        if field < 2 * count:
            tile = tracers_ref[pl.ds(field * SUB, SUB), :]
        elif field < 3 * count:
            tile = velocity_ref[pl.ds((field - 2 * count) * SUB, SUB), :]
        else:
            tile = depth
        west_pack = jnp.where(lane == field, pltpu.roll(tile, field, 1), west_pack)
        east_pack = jnp.where(lane == field, pltpu.roll(tile, field + 1, 1), east_pack)
    near_ref[at : at + SUB, :] = west_pack
    near_ref[at + SUB : at + 2 * SUB, :] = east_pack


def tracer_kernel(
    count, blocks, vdiff_ref, tracers_ref, velocity_ref, depth_ref, near_ref, far_ref, edge_ref, out_ref
):
    blk = lax.axis_index("blk")
    odd = blk % 2 == 1
    fold = blk == blocks - 1
    lane, sub = tile_iota(1), tile_iota(0)
    rows = far_ref.shape[0]
    near = near_ref[0:rows, :]
    far = jnp.where(blk == 0, 0.0, far_ref[...])
    row_id = lax.broadcasted_iota(jnp.int32, (rows, LANE), 0)
    sign = jnp.where((row_id >= 2 * count) & (row_id < 3 * count), -1.0, 1.0)
    far_north = jnp.where(fold, reversed_lanes(far) * sign, far)
    north_rows = jnp.where(odd, far_north, near)
    south_rows = jnp.where(odd, near, far)
    edge_base = edge_ref.shape[0] - 2 * SUB
    east_cols = edge_ref[edge_base : edge_base + SUB, :]
    west_cols = edge_ref[edge_base + SUB : edge_base + 2 * SUB, :]

    def spread(packed, field, at):
        return pltpu.roll(packed, (at - field) % LANE, 1)

    def east_of(tile, field):
        return jnp.where(lane == LANE - 1, spread(east_cols, field, LANE - 1), pltpu.roll(tile, LANE - 1, 1))

    def west_of(tile, field):
        return jnp.where(lane == 0, spread(west_cols, field, 0), pltpu.roll(tile, 1, 1))

    def north_of(tile, field):
        ghost = jnp.broadcast_to(north_rows[field : field + 1, :], (SUB, LANE))
        return jnp.where(sub == SUB - 1, ghost, pltpu.roll(tile, SUB - 1, 0))

    def south_of(tile, field):
        ghost = jnp.broadcast_to(south_rows[field : field + 1, :], (SUB, LANE))
        return jnp.where(sub == 0, ghost, pltpu.roll(tile, 1, 0))

    depth = depth_ref[...].astype(jnp.float32)
    at = 3 * count
    open_east = jnp.minimum(depth, east_of(depth, at))
    open_west = jnp.minimum(depth, west_of(depth, at))
    open_north = jnp.minimum(depth, north_of(depth, at))
    open_south = jnp.minimum(depth, south_of(depth, at))

    def flux(here, there, speed):
        return speed * (there + here) - MIX_COEF * (there - here)

    below = [None, None]
    for level in range(count):
        u = velocity_ref[pl.ds(level * SUB, SUB), :]
        v = velocity_ref[pl.ds((count + level) * SUB, SUB), :]
        k = float(level)
        east_speed = 0.25 * (u + east_of(u, 2 * count + level))
        west_speed = 0.25 * (u + west_of(u, 2 * count + level))
        north_speed = 0.25 * (v + north_of(v, 2 * count + level))
        south_speed = 0.25 * (v + south_of(v, 2 * count + level))
        for which in range(2):
            field = which * count + level
            here = tracers_ref[pl.ds(field * SUB, SUB), :]
            out = jnp.where(open_east > k, flux(here, east_of(here, field), east_speed), 0.0)
            out -= jnp.where(open_west > k, flux(west_of(here, field), here, west_speed), 0.0)
            out += jnp.where(open_north > k, flux(here, north_of(here, field), north_speed), 0.0)
            out -= jnp.where(open_south > k, flux(south_of(here, field), here, south_speed), 0.0)
            tendency = -out
            if level + 1 < count:
                under = tracers_ref[pl.ds((field + 1) * SUB, SUB), :]
                vertical = jnp.where(depth > k + 1.0, vdiff_ref[level] * (under - here), 0.0)
                tendency += vertical
            else:
                vertical = None
            if below[which] is not None:
                tendency -= below[which]
            below[which] = vertical
            out_ref[pl.ds(field * SUB, SUB), :] = jnp.where(depth > k, here + TIME_STEP * tendency, 0.0)


def solve_kernel(count, blocks, sources, *refs):
    *came_refs, rows_ref, surface_ref, residual_ref, rows_hbm, fields, grids, sem = refs
    leaving = pltpu.make_async_copy(rows_ref, rows_hbm, sem)
    leaving.start()
    blk, grp = lax.axis_index("blk"), lax.axis_index("grp")
    pitch = blocks + 1
    halves = range(2)

    first = (grp * (SUB * pitch), (1 - grp) * (SUB * pitch))
    for ref, masks in zip(came_refs, sources):
        for slot, mask in enumerate(masks):
            start = first[mask & 1] + (blk ^ (mask >> 1))
            for part in range(3):
                at = (slot * 3 + part) * SUB
                fields[part, pl.ds(start, SUB, stride=pitch), :] = ref[at : at + SUB, :]

    def field(part, row):
        starts = [(half * SUB + row) * pitch for half in halves]
        return [fields[part, at : at + blocks, :] for at in starts]

    residuals, applieds, alongs, easts, norths, diagonals = range(6)

    def rows_of(half, row):
        return slice((half * SUB + row) * blocks, (half * SUB + row + 1) * blocks)

    def get(which, row):
        return [grids[which, rows_of(half, row), :] for half in halves]

    def put(which, row, pair):
        for half in halves:
            grids[which, rows_of(half, row), :] = pair[half]

    def own(which):
        return grids[which, pl.ds(grp * (SUB * blocks) + blk, SUB, stride=blocks), :]

    lane = lax.broadcasted_iota(jnp.int32, (blocks, LANE), 1)
    block = lax.broadcasted_iota(jnp.int32, (blocks, LANE), 0)

    def east_of(pair):
        low, high = (pltpu.roll(half, LANE - 1, 1) for half in pair)
        return [jnp.where(lane == LANE - 1, high, low), jnp.where(lane == LANE - 1, low, high)]

    def west_of(pair):
        low, high = (pltpu.roll(half, 1, 1) for half in pair)
        return [jnp.where(lane == 0, high, low), jnp.where(lane == 0, low, high)]

    def above_last(lowest, highest, sign=1.0):
        out = []
        for half in halves:
            ghost = reversed_lanes(highest[1 - half][blocks - SUB :, :]) * sign
            moved = pltpu.roll(lowest[half], blocks - 1, 0)
            top = jnp.where(block[blocks - SUB :, :] == blocks - 1, ghost, moved[blocks - SUB :, :])
            out.append(jnp.concatenate([moved[: blocks - SUB, :], top], 0))
        return out

    def below_first(highest):
        return [jnp.where(block == 0, 0.0, pltpu.roll(half, 1, 0)) for half in highest]

    def northward(part, sign):
        sets = [field(part, row) for row in range(SUB)]
        return sets, [*sets[1:], above_last(sets[0], sets[-1], sign)]

    def total(value):
        part = value[:SUB, :]
        for at in range(SUB, blocks, SUB):
            part = part + value[at : at + SUB, :]
        for shift in (4, 2, 1):
            part = part + pltpu.roll(part, shift, 0)
        return jnp.broadcast_to(jnp.sum(part, axis=1, keepdims=True), (SUB, LANE))

    def wide(value):
        return jnp.concatenate([value] * (blocks // SUB), 0)

    def apply_op(values):
        top = above_last(values[0], values[-1])
        squares = jnp.zeros((blocks, LANE), jnp.float32)
        products = jnp.zeros((blocks, LANE), jnp.float32)

        def north_flux(row):
            north = values[row + 1] if row + 1 < SUB else top
            weight = get(norths, row)
            return [weight[half] * (north[half] - values[row][half]) for half in halves]

        last = north_flux(SUB - 1)
        flux_s = below_first(last)
        for row in range(SUB):
            x, weight, diagonal = values[row], get(easts, row), get(diagonals, row)
            east = east_of(x)
            flux_e = [weight[half] * (east[half] - x[half]) for half in halves]
            flux_w = west_of(flux_e)
            flux_n = north_flux(row) if row + 1 < SUB else last
            applied = [
                diagonal[half] * x[half] - (flux_e[half] - flux_w[half]) - (flux_n[half] - flux_s[half])
                for half in halves
            ]
            put(applieds, row, applied)
            squares += x[0] * x[0] + x[1] * x[1]
            products += x[0] * applied[0] + x[1] * applied[1]
            flux_s = flux_n
        return total(squares), total(products)

    depth, depth_n = northward(2, 1.0)
    v, v_n = northward(1, -1.0)
    v_s = below_first(v[-1])
    forcing = []
    for row in range(SUB):
        here = depth[row]
        here_e = east_of(here)
        put(easts, row, [jnp.minimum(here[half], here_e[half]) * (1.0 / count) for half in halves])
        put(norths, row, [jnp.minimum(here[half], depth_n[row][half]) * (1.0 / count) for half in halves])
        put(diagonals, row, [jnp.where(here[half] > 0.0, SEA_DIAG, 1.0) for half in halves])
        u = field(0, row)
        u_e, u_w = east_of(u), west_of(u)
        value = [
            jnp.where(here[half] > 0.0, 0.5 * (u_e[half] - u_w[half]) + 0.5 * (v_n[row][half] - v_s[half]), 0.0)
            for half in halves
        ]
        put(residuals, row, value)
        forcing.append(value)
        v_s = v[row]

    norm_now, product = apply_op(forcing)
    step_len = norm_now / product
    beta_ratio = None
    own_residual = own(residuals)
    own_along = own(applieds)
    own_direction = own_residual
    own_surface = jnp.zeros((SUB, LANE), jnp.float32)
    for sweep in range(ITERS):
        own_surface = own_surface + step_len * own_direction
        own_residual = own_residual - step_len * own_along
        if sweep + 1 < ITERS:
            values = []
            wide_step = wide(step_len)
            wide_beta = None if beta_ratio is None else wide(beta_ratio)
            for row in range(SUB):
                along, residual = get(applieds, row), get(residuals, row)
                if wide_beta is not None:
                    before = get(alongs, row)
                    along = [along[half] + wide_beta * before[half] for half in halves]
                value = [residual[half] - wide_step * along[half] for half in halves]
                if sweep + 2 < ITERS:
                    put(alongs, row, along)
                    put(residuals, row, value)
                values.append(value)
            norm_next, product = apply_op(values)
            beta_ratio = norm_next / norm_now
            step_len = norm_next / (product - beta_ratio * norm_next / step_len)
            own_direction = own_residual + beta_ratio * own_direction
            own_along = own(applieds) + beta_ratio * own_along
            norm_now = norm_next
    surface_ref[...] = own_surface
    residual_ref[...] = own_residual
    leaving.wait()


VMEM_SPEC = pl.BlockSpec(memory_space=pltpu.VMEM)
SMEM_SPEC = pl.BlockSpec(memory_space=pltpu.SMEM)
SMALL_GRANT = pltpu.CompilerParams(vmem_limit_bytes=8 << 20)


def tile_shape(rows):
    return jax.ShapeDtypeStruct((rows, LANE), jnp.float32)


def single_stages(devices):
    return [1 << bit | 2 for bit in range(devices.bit_length() - 2, 2, -1)]


def small_shards(tracers, velocity, depth_levels, vdiff):
    count = tracers.shape[1]
    blocks = lax.axis_size("blk")
    devices = blocks * 2
    rows = 2 * count * SUB
    halo_rows = 3 * count + SUB

    arguments = (tracers.reshape(rows, LANE), velocity.reshape(rows, LANE), depth_levels)
    sums, tracer_rows, velocity_rows, depth = pl.pallas_call(
        functools.partial(sums_kernel, count),
        out_shape=[
            tile_shape(3 * SUB),
            tile_shape(rows),
            tile_shape(rows),
            jax.ShapeDtypeStruct((SUB, LANE), jnp.int32),
        ],
        in_specs=[pl.BlockSpec(memory_space=pltpu.HBM)] * 3,
        out_specs=[VMEM_SPEC] * 4,
        scratch_shapes=[pltpu.SemaphoreType.DMA((3,))],
        compiler_params=SMALL_GRANT,
        name="sums",
    )(*(pltpu.with_memory_space_constraint(x, pltpu.HBM) for x in arguments))
    near, far = pl.pallas_call(
        functools.partial(pack_kernel, count),
        out_shape=[tile_shape(halo_rows + 2 * SUB), tile_shape(halo_rows)],
        in_specs=[VMEM_SPEC] * 3,
        out_specs=[VMEM_SPEC] * 2,
        compiler_params=SMALL_GRANT,
        name="pack",
    )(tracer_rows, velocity_rows, depth)

    near = lax.ppermute(near, AXES, [(i, i ^ 2) for i in range(devices)])
    far_pairs = []
    for blk in range(1, blocks, 2):
        for grp in range(2):
            here = blk * 2 + grp
            far_pairs += [(here, here ^ 1)] if blk == blocks - 1 else [(here, here + 2), (here + 2, here)]
    far = lax.ppermute(far, AXES, far_pairs + [(0, 1), (1, 0)])

    def exchanged(value, mask):
        return lax.ppermute(value, AXES, [(i, i ^ mask) for i in range(devices)])

    gathered, apart = sums, [0]
    for mask in single_stages(devices):
        gathered = jnp.concatenate([gathered, exchanged(gathered, mask)], 0)
        apart = apart + [mask ^ came for came in apart]
    both = exchanged(gathered, 7)
    crossed = exchanged(jnp.concatenate([gathered, near[halo_rows:]], 0), 3)
    second = exchanged(gathered, 6)
    straight = exchanged(gathered, 4)
    mine = jnp.concatenate([gathered, both, crossed[: gathered.shape[0]]], 0)
    theirs = exchanged(mine, 2)
    sources = (
        [came ^ mask for mask in (0, 7, 3) for came in apart],
        [came ^ mask ^ 2 for mask in (0, 7, 3) for came in apart],
        [came ^ 6 for came in apart],
        [came ^ 4 for came in apart],
    )

    new_rows = pl.pallas_call(
        functools.partial(tracer_kernel, count, blocks),
        out_shape=pltpu.VMEM((rows, LANE), jnp.float32),
        in_specs=[SMEM_SPEC] + [VMEM_SPEC] * 6,
        out_specs=VMEM_SPEC,
        compiler_params=SMALL_GRANT,
        name="tracer",
    )(vdiff, tracer_rows, velocity_rows, depth, near, far, crossed)

    surface, residual, new_rows = pl.pallas_call(
        functools.partial(solve_kernel, count, blocks, sources),
        out_shape=[tile_shape(SUB), tile_shape(SUB), tile_shape(rows)],
        in_specs=[VMEM_SPEC] * 5,
        out_specs=[VMEM_SPEC, VMEM_SPEC, pl.BlockSpec(memory_space=pltpu.HBM)],
        scratch_shapes=[
            pltpu.VMEM((3, 2 * SUB * (blocks + 1), LANE), jnp.float32),
            pltpu.VMEM((6, 2 * SUB * blocks, LANE), jnp.float32),
            pltpu.SemaphoreType.DMA,
        ],
        compiler_params=SMALL_GRANT,
        name="solve",
    )(mine, theirs, second, straight, new_rows)
    return new_rows.reshape(tracers.shape), surface, residual


def shards(tracers, velocity, depth_levels, vdiff):
    blocks, groups = lax.axis_size("blk"), lax.axis_size("grp")
    height, breadth = depth_levels.shape
    tiled = (height, breadth) == (SUB, LANE) and groups == 2 and blocks >= SUB and blocks & (blocks - 1) == 0
    if tiled and 3 * tracers.shape[1] < LANE and blocks * groups * SUB * LANE <= GATHER_CELLS:
        return small_shards(tracers, velocity, depth_levels, vdiff)
    return wide_shards(tracers, velocity, depth_levels, vdiff)


def solution(mesh):
    return jax.shard_map(
        shards,
        mesh=mesh,
        in_specs=(P(None, None, "blk", "grp"), P(None, None, "blk", "grp"), P("blk", "grp"), P()),
        out_specs=(P(None, None, "blk", "grp"), P("blk", "grp"), P("blk", "grp")),
        check_vma=False,
    )
```

```python
import functools

import jax
import jax.numpy as jnp
from jax import lax
from jax.experimental import pallas as pl
from jax.experimental.pallas import tpu as pltpu
from jax.sharding import PartitionSpec as P


ITERS = 3


TIME_STEP = 0.2
MIX_COEF = 0.25
SEA_DIAG = 0.5

AXES = ("blk", "grp")
GATHER_CELLS = 1 << 17


def swapped(value, axis, stride):
    return lax.ppermute(value, axis, [(i, i ^ 1 << stride) for i in range(lax.axis_size(axis))])


def padded_2(cells, sides, width, closed):
    for axis, dim in sides:
        count = lax.axis_size(axis)
        ends = count if closed else count - 1
        head = lax.slice_in_dim(cells, 0, width, axis=dim)
        tail = lax.slice_in_dim(cells, cells.shape[dim] - width, cells.shape[dim], axis=dim)
        cells = jnp.concatenate(
            [
                lax.ppermute(tail, axis, [(i, (i + 1) % count) for i in range(ends)]),
                cells,
                lax.ppermute(head, axis, [((i + 1) % count, i) for i in range(ends)]),
            ],
            axis=dim,
        )
    return cells


def tracer_step(tracer, velocity, depth_pad, vdiff):
    count = tracer.shape[1]
    levels = jnp.arange(count, dtype=jnp.float32)[:, None, None]
    wet_mask = (levels < depth_pad[None]).astype(jnp.float32)
    east_vel = velocity[0]
    north_vel = velocity[1]
    row_set = tracer[:, :, 1:-1, :]
    wet_rows = wet_mask[:, 1:-1, :]
    east_rows = east_vel[:, 1:-1, :]
    east_open = wet_rows[:, :, :-1] * wet_rows[:, :, 1:]
    east_face = 0.5 * (east_rows[:, :, :-1] + east_rows[:, :, 1:])
    east_flux = east_open * (
        east_face * 0.5 * (row_set[..., :-1] + row_set[..., 1:])
        - MIX_COEF * (row_set[..., 1:] - row_set[..., :-1])
    )
    col_set = tracer[:, :, :, 1:-1]
    wet_cols = wet_mask[:, :, 1:-1]
    north_cols = north_vel[:, :, 1:-1]
    north_open = wet_cols[:, :-1, :] * wet_cols[:, 1:, :]
    north_face = 0.5 * (north_cols[:, :-1, :] + north_cols[:, 1:, :])
    north_flux = north_open * (
        north_face * 0.5 * (col_set[:, :, :-1, :] + col_set[:, :, 1:, :])
        - MIX_COEF * (col_set[:, :, 1:, :] - col_set[:, :, :-1, :])
    )
    centre = tracer[:, :, 1:-1, 1:-1]
    wet_centre = wet_mask[:, 1:-1, 1:-1]
    vert_open = wet_centre[:-1] * wet_centre[1:]
    vert_flux = vdiff[:, None, None] * vert_open * (centre[:, 1:] - centre[:, :-1])
    border = jnp.zeros_like(centre[:, :1])
    vert_flux = jnp.concatenate([border, vert_flux, border], 1)
    tendency = (
        vert_flux[:, 1:]
        - vert_flux[:, :-1]
        - (east_flux[..., 1:] - east_flux[..., :-1])
        - (north_flux[:, :, 1:, :] - north_flux[:, :, :-1, :])
    )
    return wet_centre * (centre + TIME_STEP * tendency)


def column_forcing(velocity, depth_pad):
    count = velocity.shape[1]
    levels = jnp.arange(count, dtype=jnp.float32)[:, None, None]
    wet_mask = (levels < depth_pad[None]).astype(jnp.float32)
    east_sum = jnp.sum(wet_mask * velocity[0], 0)
    north_sum = jnp.sum(wet_mask * velocity[1], 0)
    ocean_mask = (depth_pad[1:-1, 1:-1] > 0).astype(jnp.float32)
    return ocean_mask * (
        0.5 * (east_sum[1:-1, 2:] - east_sum[1:-1, :-2])
        + 0.5 * (north_sum[2:, 1:-1] - north_sum[:-2, 1:-1])
    )


def sea_operator(field_pad, depth_pad, count):
    centre = field_pad[1:-1, 1:-1]
    depth_c = depth_pad[1:-1, 1:-1]
    ocean_mask = (depth_c > 0).astype(jnp.float32)
    total = SEA_DIAG * centre
    for rows_at, cols_at in (
        (slice(1, -1), slice(2, None)),
        (slice(1, -1), slice(None, -2)),
        (slice(2, None), slice(1, -1)),
        (slice(None, -2), slice(1, -1)),
    ):
        weight = jnp.minimum(depth_c, depth_pad[rows_at, cols_at]) / count
        total = total + weight * (centre - field_pad[rows_at, cols_at])
    return ocean_mask * total + (1.0 - ocean_mask) * centre


def extend(fields, fold_sign):
    top_row = fields[:, -1, :]
    partner = top_row
    for bit_index in range(lax.axis_size("grp").bit_length() - 1):
        partner = swapped(partner, "grp", bit_index)
    mirror = partner[:, ::-1]
    northmost = lax.axis_index("blk") == lax.axis_size("blk") - 1
    row_halo = padded_2(fields, (("blk", 1),), 1, False)
    north_row = jnp.where(northmost, mirror * fold_sign[:, None], row_halo[:, -1, :])
    grown = jnp.concatenate([row_halo[:, :-1, :], north_row[:, None, :]], 1)
    return padded_2(grown, (("grp", 2),), 1, True)


def two_sums(residual, applied):
    return lax.psum((jnp.sum(residual * residual), jnp.sum(residual * applied)), AXES)


def wide_shards(tracers, velocity, depth_levels, vdiff):
    count = tracers.shape[1]
    height, breadth = depth_levels.shape
    fields = jnp.concatenate(
        [
            tracers.reshape(2 * count, height, breadth),
            velocity.reshape(2 * count, height, breadth),
            depth_levels.astype(jnp.float32)[None],
        ],
        0,
    )
    fold_sign = jnp.concatenate(
        [
            jnp.ones((2 * count,), jnp.float32),
            -jnp.ones((2 * count,), jnp.float32),
            jnp.ones((1,), jnp.float32),
        ]
    )
    padded = extend(fields, fold_sign)
    tracer_pad = padded[: 2 * count].reshape(2, count, height + 2, breadth + 2)
    velocity_pad = padded[2 * count : 4 * count].reshape(2, count, height + 2, breadth + 2)
    depth_pad = padded[4 * count]
    new_tracers = tracer_step(tracer_pad, velocity_pad, depth_pad, vdiff)
    forcing = column_forcing(velocity_pad, depth_pad)

    def apply_op(field):
        grown = extend(field[None], jnp.ones((1,), jnp.float32))[0]
        return sea_operator(grown, depth_pad, count)

    surface = jnp.zeros_like(forcing)
    residual = forcing
    applied = apply_op(residual)
    norm_now, product = two_sums(residual, applied)
    step_len = norm_now / product
    direction, along = (residual, applied)
    for sweep in range(ITERS):
        surface = surface + step_len * direction
        residual = residual - step_len * along
        if sweep + 1 < ITERS:
            applied = apply_op(residual)
            norm_next, product = two_sums(residual, applied)
            beta_ratio = norm_next / norm_now
            step_len = norm_next / (product - beta_ratio * norm_next / step_len)
            direction = residual + beta_ratio * direction
            along = applied + beta_ratio * along
            norm_now = norm_next
    return (new_tracers, surface, residual)


SUB, LANE = 8, 128


def tile_iota(dim):
    return lax.broadcasted_iota(jnp.int32, (SUB, LANE), dim)


def reversed_lanes(value):
    index = LANE - 1 - lax.broadcasted_iota(jnp.int32, value.shape, 1)
    return jnp.take_along_axis(value, index, axis=1)


def sums_kernel(count, tracers_hbm, velocity_hbm, depth_hbm, sums_ref, tracers_ref, velocity_ref, depth_ref, sems):
    copies = [
        pltpu.make_async_copy(src, dst, sems.at[at])
        for at, (src, dst) in enumerate(
            ((depth_hbm, depth_ref), (velocity_hbm, velocity_ref), (tracers_hbm, tracers_ref))
        )
    ]
    for copy in copies:
        copy.start()
    copies[0].wait()
    copies[1].wait()
    depth = depth_ref[...]
    east = jnp.zeros((SUB, LANE), jnp.float32)
    north = jnp.zeros((SUB, LANE), jnp.float32)
    for level in range(count):
        wet = depth > level
        east += jnp.where(wet, velocity_ref[pl.ds(level * SUB, SUB), :], 0.0)
        north += jnp.where(wet, velocity_ref[pl.ds((count + level) * SUB, SUB), :], 0.0)
    sums_ref[0:SUB, :] = east
    sums_ref[SUB : 2 * SUB, :] = north
    sums_ref[2 * SUB : 3 * SUB, :] = depth.astype(jnp.float32)
    copies[2].wait()


def pack_kernel(count, tracers_ref, velocity_ref, depth_ref, near_ref, far_ref):
    odd = lax.axis_index("blk") % 2 == 1
    depth = depth_ref[...].astype(jnp.float32)

    def both(ref, first, rows):
        low = ref[pl.ds(first, rows, stride=SUB), :]
        high = ref[pl.ds(first + SUB - 1, rows, stride=SUB), :]
        return jnp.where(odd, low, high), jnp.where(odd, high, low)

    depth_low = jnp.broadcast_to(depth[0:1, :], (SUB, LANE))
    depth_high = jnp.broadcast_to(depth[SUB - 1 : SUB, :], (SUB, LANE))
    parts = (
        both(tracers_ref, 0, 2 * count),
        both(velocity_ref, count * SUB, count),
        (jnp.where(odd, depth_low, depth_high), jnp.where(odd, depth_high, depth_low)),
    )
    at = 0
    for near, far in parts:
        near_ref[at : at + near.shape[0], :] = near
        far_ref[at : at + near.shape[0], :] = far
        at += near.shape[0]
    lane = tile_iota(1)
    pack = jnp.zeros((SUB, LANE), jnp.float32)
    for field in range(3 * count + 1):
        if field < 2 * count:
            tile = tracers_ref[pl.ds(field * SUB, SUB), :]
        elif field < 3 * count:
            tile = velocity_ref[pl.ds((field - 2 * count) * SUB, SUB), :]
        else:
            tile = depth
        pack = jnp.where(lane == field, pltpu.roll(tile, field, 1), pack)
        pack = jnp.where(lane == LANE // 2 + field, pltpu.roll(tile, LANE // 2 + field + 1, 1), pack)
    near_ref[at : at + SUB, :] = pack


def tracer_kernel(
    count, blocks, vdiff_ref, tracers_ref, velocity_ref, depth_ref, near_ref, far_ref, edge_ref, out_ref
):
    blk = lax.axis_index("blk")
    odd = blk % 2 == 1
    fold = blk == blocks - 1
    lane, sub = tile_iota(1), tile_iota(0)
    rows = far_ref.shape[0]
    near = near_ref[0:rows, :]
    far = jnp.where(blk == 0, 0.0, far_ref[...])
    row_id = lax.broadcasted_iota(jnp.int32, (rows, LANE), 0)
    sign = jnp.where((row_id >= 2 * count) & (row_id < 3 * count), -1.0, 1.0)
    far_north = jnp.where(fold, reversed_lanes(far) * sign, far)
    north_rows = jnp.where(odd, far_north, near)
    south_rows = jnp.where(odd, near, far)
    columns = edge_ref[edge_ref.shape[0] - SUB :, :]

    def spread(first, at):
        return pltpu.roll(columns, (at - first) % LANE, 1)

    def east_of(tile, field):
        return jnp.where(lane == LANE - 1, spread(field, LANE - 1), pltpu.roll(tile, LANE - 1, 1))

    def west_of(tile, field):
        return jnp.where(lane == 0, spread(LANE // 2 + field, 0), pltpu.roll(tile, 1, 1))

    def north_of(tile, field):
        ghost = jnp.broadcast_to(north_rows[field : field + 1, :], (SUB, LANE))
        return jnp.where(sub == SUB - 1, ghost, pltpu.roll(tile, SUB - 1, 0))

    def south_of(tile, field):
        ghost = jnp.broadcast_to(south_rows[field : field + 1, :], (SUB, LANE))
        return jnp.where(sub == 0, ghost, pltpu.roll(tile, 1, 0))

    depth = depth_ref[...].astype(jnp.float32)
    at = 3 * count
    open_east = jnp.minimum(depth, east_of(depth, at))
    open_west = jnp.minimum(depth, west_of(depth, at))
    open_north = jnp.minimum(depth, north_of(depth, at))
    open_south = jnp.minimum(depth, south_of(depth, at))

    def flux(here, there, speed):
        return speed * (there + here) - MIX_COEF * (there - here)

    below = [None, None]
    for level in range(count):
        u = velocity_ref[pl.ds(level * SUB, SUB), :]
        v = velocity_ref[pl.ds((count + level) * SUB, SUB), :]
        k = float(level)
        east_speed = 0.25 * (u + east_of(u, 2 * count + level))
        west_speed = 0.25 * (u + west_of(u, 2 * count + level))
        north_speed = 0.25 * (v + north_of(v, 2 * count + level))
        south_speed = 0.25 * (v + south_of(v, 2 * count + level))
        for which in range(2):
            field = which * count + level
            here = tracers_ref[pl.ds(field * SUB, SUB), :]
            out = jnp.where(open_east > k, flux(here, east_of(here, field), east_speed), 0.0)
            out -= jnp.where(open_west > k, flux(west_of(here, field), here, west_speed), 0.0)
            out += jnp.where(open_north > k, flux(here, north_of(here, field), north_speed), 0.0)
            out -= jnp.where(open_south > k, flux(south_of(here, field), here, south_speed), 0.0)
            tendency = -out
            if level + 1 < count:
                under = tracers_ref[pl.ds((field + 1) * SUB, SUB), :]
                vertical = jnp.where(depth > k + 1.0, vdiff_ref[level] * (under - here), 0.0)
                tendency += vertical
            else:
                vertical = None
            if below[which] is not None:
                tendency -= below[which]
            below[which] = vertical
            out_ref[pl.ds(field * SUB, SUB), :] = jnp.where(depth > k, here + TIME_STEP * tendency, 0.0)


def solve_kernel(count, blocks, sources, *refs):
    *came_refs, rows_ref, surface_ref, residual_ref, rows_hbm, fields, grids, sem = refs
    leaving = pltpu.make_async_copy(rows_ref, rows_hbm, sem)
    leaving.start()
    blk, grp = lax.axis_index("blk"), lax.axis_index("grp")
    pitch = blocks + 1
    halves = range(2)

    first = (grp * (SUB * pitch), (1 - grp) * (SUB * pitch))
    for ref, masks in zip(came_refs, sources):
        for slot, mask in enumerate(masks):
            start = first[mask & 1] + (blk ^ (mask >> 1))
            for part in range(3):
                at = (slot * 3 + part) * SUB
                fields[part, pl.ds(start, SUB, stride=pitch), :] = ref[at : at + SUB, :]

    def field(part, row):
        starts = [(half * SUB + row) * pitch for half in halves]
        return [fields[part, at : at + blocks, :] for at in starts]

    residuals, applieds, alongs, easts, norths, diagonals = range(6)

    def rows_of(half, row):
        return slice((half * SUB + row) * blocks, (half * SUB + row + 1) * blocks)

    def get(which, row):
        return [grids[which, rows_of(half, row), :] for half in halves]

    def put(which, row, pair):
        for half in halves:
            grids[which, rows_of(half, row), :] = pair[half]

    def own(which):
        return grids[which, pl.ds(grp * (SUB * blocks) + blk, SUB, stride=blocks), :]

    lane = lax.broadcasted_iota(jnp.int32, (blocks, LANE), 1)
    block = lax.broadcasted_iota(jnp.int32, (blocks, LANE), 0)

    def east_of(pair):
        low, high = (pltpu.roll(half, LANE - 1, 1) for half in pair)
        return [jnp.where(lane == LANE - 1, high, low), jnp.where(lane == LANE - 1, low, high)]

    def west_of(pair):
        low, high = (pltpu.roll(half, 1, 1) for half in pair)
        return [jnp.where(lane == 0, high, low), jnp.where(lane == 0, low, high)]

    def above_last(lowest, highest, sign=1.0):
        out = []
        for half in halves:
            ghost = reversed_lanes(highest[1 - half][blocks - SUB :, :]) * sign
            moved = pltpu.roll(lowest[half], blocks - 1, 0)
            top = jnp.where(block[blocks - SUB :, :] == blocks - 1, ghost, moved[blocks - SUB :, :])
            out.append(jnp.concatenate([moved[: blocks - SUB, :], top], 0))
        return out

    def below_first(highest):
        return [jnp.where(block == 0, 0.0, pltpu.roll(half, 1, 0)) for half in highest]

    def northward(part, sign):
        sets = [field(part, row) for row in range(SUB)]
        return sets, [*sets[1:], above_last(sets[0], sets[-1], sign)]

    def total(value):
        part = value[:SUB, :]
        for at in range(SUB, blocks, SUB):
            part = part + value[at : at + SUB, :]
        for shift in (4, 2, 1):
            part = part + pltpu.roll(part, shift, 0)
        return jnp.broadcast_to(jnp.sum(part, axis=1, keepdims=True), (SUB, LANE))

    def wide(value):
        return jnp.concatenate([value] * (blocks // SUB), 0)

    def apply_op(values):
        top = above_last(values[0], values[-1])
        squares = jnp.zeros((blocks, LANE), jnp.float32)
        products = jnp.zeros((blocks, LANE), jnp.float32)

        def north_flux(row):
            north = values[row + 1] if row + 1 < SUB else top
            weight = get(norths, row)
            return [weight[half] * (north[half] - values[row][half]) for half in halves]

        last = north_flux(SUB - 1)
        flux_s = below_first(last)
        for row in range(SUB):
            x, weight, diagonal = values[row], get(easts, row), get(diagonals, row)
            east = east_of(x)
            flux_e = [weight[half] * (east[half] - x[half]) for half in halves]
            flux_w = west_of(flux_e)
            flux_n = north_flux(row) if row + 1 < SUB else last
            applied = [
                diagonal[half] * x[half] - (flux_e[half] - flux_w[half]) - (flux_n[half] - flux_s[half])
                for half in halves
            ]
            put(applieds, row, applied)
            squares += x[0] * x[0] + x[1] * x[1]
            products += x[0] * applied[0] + x[1] * applied[1]
            flux_s = flux_n
        return total(squares), total(products)

    depth, depth_n = northward(2, 1.0)
    v, v_n = northward(1, -1.0)
    v_s = below_first(v[-1])
    forcing = []
    for row in range(SUB):
        here = depth[row]
        here_e = east_of(here)
        put(easts, row, [jnp.minimum(here[half], here_e[half]) * (1.0 / count) for half in halves])
        put(norths, row, [jnp.minimum(here[half], depth_n[row][half]) * (1.0 / count) for half in halves])
        put(diagonals, row, [jnp.where(here[half] > 0.0, SEA_DIAG, 1.0) for half in halves])
        u = field(0, row)
        u_e, u_w = east_of(u), west_of(u)
        value = [
            jnp.where(here[half] > 0.0, 0.5 * (u_e[half] - u_w[half]) + 0.5 * (v_n[row][half] - v_s[half]), 0.0)
            for half in halves
        ]
        put(residuals, row, value)
        forcing.append(value)
        v_s = v[row]

    norm_now, product = apply_op(forcing)
    step_len = norm_now / product
    beta_ratio = None
    own_residual = own(residuals)
    own_along = own(applieds)
    own_direction = own_residual
    own_surface = jnp.zeros((SUB, LANE), jnp.float32)
    for sweep in range(ITERS):
        own_surface = own_surface + step_len * own_direction
        own_residual = own_residual - step_len * own_along
        if sweep + 1 < ITERS:
            values = []
            wide_step = wide(step_len)
            wide_beta = None if beta_ratio is None else wide(beta_ratio)
            for row in range(SUB):
                along, residual = get(applieds, row), get(residuals, row)
                if wide_beta is not None:
                    before = get(alongs, row)
                    along = [along[half] + wide_beta * before[half] for half in halves]
                value = [residual[half] - wide_step * along[half] for half in halves]
                if sweep + 2 < ITERS:
                    put(alongs, row, along)
                    put(residuals, row, value)
                values.append(value)
            norm_next, product = apply_op(values)
            beta_ratio = norm_next / norm_now
            step_len = norm_next / (product - beta_ratio * norm_next / step_len)
            own_direction = own_residual + beta_ratio * own_direction
            own_along = own(applieds) + beta_ratio * own_along
            norm_now = norm_next
    surface_ref[...] = own_surface
    residual_ref[...] = own_residual
    leaving.wait()


VMEM_SPEC = pl.BlockSpec(memory_space=pltpu.VMEM)
SMEM_SPEC = pl.BlockSpec(memory_space=pltpu.SMEM)
SMALL_GRANT = pltpu.CompilerParams(vmem_limit_bytes=8 << 20)


def tile_shape(rows):
    return jax.ShapeDtypeStruct((rows, LANE), jnp.float32)


def single_stages(devices):
    return [1 << bit | 2 for bit in range(devices.bit_length() - 2, 2, -1)]


def small_shards(tracers, velocity, depth_levels, vdiff):
    count = tracers.shape[1]
    blocks = lax.axis_size("blk")
    devices = blocks * 2
    rows = 2 * count * SUB
    halo_rows = 3 * count + SUB

    arguments = (tracers.reshape(rows, LANE), velocity.reshape(rows, LANE), depth_levels)
    sums, tracer_rows, velocity_rows, depth = pl.pallas_call(
        functools.partial(sums_kernel, count),
        out_shape=[
            tile_shape(3 * SUB),
            tile_shape(rows),
            tile_shape(rows),
            jax.ShapeDtypeStruct((SUB, LANE), jnp.int32),
        ],
        in_specs=[pl.BlockSpec(memory_space=pltpu.HBM)] * 3,
        out_specs=[VMEM_SPEC] * 4,
        scratch_shapes=[pltpu.SemaphoreType.DMA((3,))],
        compiler_params=SMALL_GRANT,
        name="sums",
    )(*(pltpu.with_memory_space_constraint(x, pltpu.HBM) for x in arguments))
    near, far = pl.pallas_call(
        functools.partial(pack_kernel, count),
        out_shape=[tile_shape(halo_rows + SUB), tile_shape(halo_rows)],
        in_specs=[VMEM_SPEC] * 3,
        out_specs=[VMEM_SPEC] * 2,
        compiler_params=SMALL_GRANT,
        name="pack",
    )(tracer_rows, velocity_rows, depth)

    near = lax.ppermute(near, AXES, [(i, i ^ 2) for i in range(devices)])
    far_pairs = []
    for blk in range(1, blocks, 2):
        for grp in range(2):
            here = blk * 2 + grp
            far_pairs += [(here, here ^ 1)] if blk == blocks - 1 else [(here, here + 2), (here + 2, here)]
    far = lax.ppermute(far, AXES, far_pairs + [(0, 1), (1, 0)])

    def exchanged(value, mask):
        return lax.ppermute(value, AXES, [(i, i ^ mask) for i in range(devices)])

    gathered, apart = sums, [0]
    for mask in single_stages(devices):
        gathered = jnp.concatenate([gathered, exchanged(gathered, mask)], 0)
        apart = apart + [mask ^ came for came in apart]
    both = exchanged(gathered, 7)
    crossed = exchanged(jnp.concatenate([gathered, near[halo_rows:]], 0), 3)
    second = exchanged(gathered, 6)
    straight = exchanged(gathered, 4)
    mine = jnp.concatenate([gathered, both, crossed[: gathered.shape[0]]], 0)
    theirs = exchanged(mine, 2)
    sources = (
        [came ^ mask for mask in (0, 7, 3) for came in apart],
        [came ^ mask ^ 2 for mask in (0, 7, 3) for came in apart],
        [came ^ 6 for came in apart],
        [came ^ 4 for came in apart],
    )

    new_rows = pl.pallas_call(
        functools.partial(tracer_kernel, count, blocks),
        out_shape=pltpu.VMEM((rows, LANE), jnp.float32),
        in_specs=[SMEM_SPEC] + [VMEM_SPEC] * 6,
        out_specs=VMEM_SPEC,
        compiler_params=SMALL_GRANT,
        name="tracer",
    )(vdiff, tracer_rows, velocity_rows, depth, near, far, crossed)

    surface, residual, new_rows = pl.pallas_call(
        functools.partial(solve_kernel, count, blocks, sources),
        out_shape=[tile_shape(SUB), tile_shape(SUB), tile_shape(rows)],
        in_specs=[VMEM_SPEC] * 5,
        out_specs=[VMEM_SPEC, VMEM_SPEC, pl.BlockSpec(memory_space=pltpu.HBM)],
        scratch_shapes=[
            pltpu.VMEM((3, 2 * SUB * (blocks + 1), LANE), jnp.float32),
            pltpu.VMEM((6, 2 * SUB * blocks, LANE), jnp.float32),
            pltpu.SemaphoreType.DMA,
        ],
        compiler_params=SMALL_GRANT,
        name="solve",
    )(mine, theirs, second, straight, new_rows)
    return new_rows.reshape(tracers.shape), surface, residual


def shards(tracers, velocity, depth_levels, vdiff):
    blocks, groups = lax.axis_size("blk"), lax.axis_size("grp")
    height, breadth = depth_levels.shape
    tiled = (height, breadth) == (SUB, LANE) and groups == 2 and blocks >= SUB and blocks & (blocks - 1) == 0
    if tiled and 3 * tracers.shape[1] < LANE // 2 and blocks * groups * SUB * LANE <= GATHER_CELLS:
        return small_shards(tracers, velocity, depth_levels, vdiff)
    return wide_shards(tracers, velocity, depth_levels, vdiff)


def solution(mesh):
    return jax.shard_map(
        shards,
        mesh=mesh,
        in_specs=(P(None, None, "blk", "grp"), P(None, None, "blk", "grp"), P("blk", "grp"), P()),
        out_specs=(P(None, None, "blk", "grp"), P("blk", "grp"), P("blk", "grp")),
        check_vma=False,
    )
```
